256 devices in a mesh: expert: 64 (over y, z, core), ctx: 4 (over x).
Axes of the slice: x: 4, y: 4, z: 8, core: 2. Of those that a mesh axis runs over, the one named last changes fastest.
Arguments:
- resid: bfloat16 [32768, 2048], P(('expert', 'ctx')), may hold values from -30 to 30
- queries: bfloat16 [32768, 2048], P(('expert', 'ctx')), may hold values from -8 to 8
- keys: bfloat16 [32768, 2048], P(('expert', 'ctx')), may hold values from -8 to 8
- values: bfloat16 [32768, 2048], P(('expert', 'ctx')), may hold values from -6 to 6
- mod_scale: float32 [64, 2048], P('expert'), may hold values from -0.5 to 0.5
- mod_shift: float32 [64, 2048], P('expert'), may hold values from -3 to 3
- mod_gate: float32 [64, 2048], P('expert'), may hold values from 0.5 to 1.5
- router: bfloat16 [2048, 64], replicated, may hold values from -0.125 to 0.125
- w_in: bfloat16 [64, 2048, 1024], P('expert', None, 'ctx'), may hold values from -0.125 to 0.125
- w_out: bfloat16 [64, 1024, 2048], P('expert', 'ctx'), may hold values from -0.1875 to 0.1875
- expert_ids: int32 [32768, 2], P(('expert', 'ctx')), may hold values from 0 to 63, all different within a row; in each aligned block of 128 rows (0 to 127, 128 to 255, ...) at most 5 rows name the same one
- grad_out: bfloat16 [32768, 2048], P(('expert', 'ctx')), may hold values from -1.5 to 1.5
Outputs:
- mixed_out: bfloat16 [32768, 2048], P(('expert', 'ctx'))
- resid_grad: bfloat16 [32768, 2048], P(('expert', 'ctx'))
- grad_queries: bfloat16 [32768, 2048], P(('expert', 'ctx'))
- grad_keys: bfloat16 [32768, 2048], P(('expert', 'ctx'))
- grad_values: bfloat16 [32768, 2048], P(('expert', 'ctx'))
- grad_w_in: bfloat16 [64, 2048, 1024], P('expert', None, 'ctx')
- grad_w_out: bfloat16 [64, 1024, 2048], P('expert', 'ctx')
- grad_router: float32 [2048, 64], replicated
The draws below stay inside these ranges and needn't reach their ends.
Inputs may be any that keep to these rules, and one draw needn't show every extreme that they name: `expert_ids`: each token names two different experts. Within one aligned block of 128 tokens no expert is named by more than 5 tokens, and some block reaches 5.
All inputs are finite; a program needn't handle non-finite values.
Results may differ from the reference program's by a relative error of at most 0.013.
The reference program's roundings to bfloat16 on the way count: a program that leaves them out, or rounds other values in their place, can miss the bound.
Values may be sent and summed in bfloat16 or wider, within the bound.
No kernel may reach another device: no remote copies, remote signals or barrier semaphores. Data moves between devices by JAX's collectives and lax.ppermute only.
A program may use at most 128 MiB of HBM per device.

```python
import math
import jax
import jax.numpy as jnp
import numpy as np
from jax import lax

D = 2048
HEADS = 16
HDIM = 128
FF = 1024
EXPERTS = 64
TOK_DEV = 128
CLIP = 512
CLIPS = 64
TOKENS = 32768
CAP = 5
FF_BLOCK = 256
N_CTX = 4


def draw_resid(key, part):
    row_key, col_key, base_key = jax.random.split(key, 3)
    row_scale = jnp.exp(jax.random.uniform(row_key, (TOKENS, 1), minval=math.log(0.25), maxval=math.log(2.5)))
    col_scale = jnp.exp(jax.random.uniform(col_key, (1, D), minval=math.log(0.3), maxval=math.log(3.0)))
    base_values = jax.random.normal(base_key, (TOKENS, D))
    return jnp.clip(base_values * row_scale * col_scale, -30.0, 30.0).astype(jnp.bfloat16)


def paired_heads(key):
    folded = jax.random.fold_in(key, 11)
    split_keys = jax.random.split(folded, 2)
    query_values = jnp.clip(jax.random.normal(split_keys[0], (TOKENS, D)), -8.0, 8.0)
    key_values = jnp.clip(jax.random.normal(split_keys[1], (TOKENS, D)), -8.0, 8.0)
    return (query_values.astype(jnp.bfloat16), key_values.astype(jnp.bfloat16))


def draw_queries(key, part):
    return paired_heads(key)[0]


def draw_keys(key, part):
    return paired_heads(key)[1]


def shard_levels(stream_key, extent, cuts, low, top_value):
    factor_of = 1.0
    for dim, shards_of in cuts:
        draws = jax.random.uniform(jax.random.fold_in(jax.random.fold_in(stream_key, 6), dim), (shards_of,), jnp.float32, low / len(cuts), top_value / len(cuts))
        factor_of = factor_of * jnp.repeat(jnp.exp(draws), extent[dim] // shards_of).reshape((-1,) + (1,) * (len(extent) - 1 - dim))
    return factor_of


def routed_block(stream_key, own, number, rows, amount, top, bound, skew):
    order = jax.random.permutation(stream_key, amount)
    heavy_load, ordinary = shares(amount, rows * top, bound, skew, True), shares(amount, rows * top, bound, skew, False)
    places = jnp.arange(amount)

    def named(tallies, turn):
        used = int((tallies > 0).sum())
        fixed = max(1, used // 4)
        shifted = fixed + (places - fixed + turn * (used - fixed)) % max(1, amount - fixed)
        return jnp.zeros((amount,), jnp.int32).at[order[jnp.where(places < fixed, places, shifted)]].set(jnp.asarray(tallies, jnp.int32))

    tallies = jnp.where(number % 4 == 0, named(heavy_load, number // 4), named(ordinary, number - number // 4 - 1))
    mixed = jax.random.permutation(jax.random.fold_in(own, 3), amount)
    giver, taker = mixed[0:amount // 2 * 2:2], mixed[1:amount // 2 * 2:2]
    room = jnp.minimum(tallies[giver] - 1, bound - tallies[taker]) // 2
    room = jnp.where((giver == order[0]) | (taker == order[0]) | (tallies[taker] == 0), 0, jnp.maximum(room, 0))
    shifted = jax.random.randint(jax.random.fold_in(own, 4), (amount // 2,), 0, 1 << 20) % (room + 1)
    tallies = tallies.at[giver].add(-shifted).at[taker].add(shifted)
    members = jnp.searchsorted(jnp.cumsum(tallies), jnp.arange(rows * top), side="right").astype(jnp.int32)
    table = members.reshape(top, rows).T
    table = table[jax.random.permutation(jax.random.fold_in(own, 1), rows)]
    turn = jax.random.randint(jax.random.fold_in(own, 2), (rows, 1), 0, top)
    return jnp.take_along_axis(table, (jnp.arange(top)[None, :] + turn) % top, axis=1)


def shares(number_of, total, reach, skew, full):
    portions = [(1 << 20) // math.isqrt(grade ** skew) + 1 for grade in range(1, number_of + 1)]
    largest = reach if full else min(reach, max(-(-total // number_of), total * portions[0] // sum(portions)))
    least = 1 if total - largest >= number_of - 1 else 0
    counts, spare = [largest] + [least] * (number_of - 1), total - largest - least * (number_of - 1)
    while spare > 0:
        candidates = [i for i in range(1, number_of) if counts[i] < largest] or [i for i in range(1, number_of) if counts[i] < reach]
        whole, remaining = sum([portions[i] for i in candidates]), spare
        for i in candidates:
            extra = min(reach - counts[i], max(1, remaining * portions[i] // whole), spare)
            counts[i] = counts[i] + extra
            spare = spare - extra
    return np.array(counts)


def centred(stream_key, dims, spread, reach, cuts=(), kind=jnp.bfloat16):
    factor_of = shard_levels(stream_key, dims, cuts, -0.22, 0.18) if cuts else 1.0
    drawn = jax.random.normal(stream_key, dims, jnp.float32) * spread * factor_of
    return jnp.minimum(jnp.maximum(drawn, -reach), reach).astype(kind)


def setup_inputs(seed: int = 0) -> dict:
    arg_keys = jax.random.split(jax.random.key(seed), 13)
    resid = draw_resid(jax.random.fold_in(arg_keys[12], 71), 0)
    queries = draw_queries(jax.random.fold_in(arg_keys[12], 71), 0)
    keys = draw_keys(jax.random.fold_in(arg_keys[12], 71), 0)
    values = centred(arg_keys[3], (TOKENS, D), 1.0, 6.0, ((0, 256),))
    mod_scale = jnp.clip(jax.random.uniform(arg_keys[4], (CLIPS, D), jnp.float32, -0.5, 0.5) * shard_levels(arg_keys[4], (CLIPS, D), ((0, 64),), -0.4, 0.0), -0.5, 0.5)
    mod_shift = centred(arg_keys[5], (CLIPS, D), 0.5, 3.0, ((0, 64),), jnp.float32)
    mod_gate = jnp.clip(0.5 + 1.0 * jax.random.uniform(arg_keys[6], (CLIPS, D), jnp.float32) ** shard_levels(arg_keys[6], (CLIPS, D), ((0, 64),), -0.2, 0.2), 0.5, 1.5)
    router = centred(arg_keys[7], (D, EXPERTS), D ** -0.5, 0.125)
    w_in = centred(arg_keys[8], (EXPERTS, D, FF), D ** -0.5, 0.125, ((0, 64), (2, 4)))
    w_out = centred(arg_keys[9], (EXPERTS, FF, D), FF ** -0.5, 0.1875, ((0, 64), (1, 4)))
    expert_ids_keys = jax.random.split(jax.random.fold_in(arg_keys[10], 1), TOKENS // TOK_DEV)
    expert_ids_turns = jax.random.permutation(jax.random.fold_in(arg_keys[10], 3), TOKENS // TOK_DEV)
    expert_ids = jax.vmap(lambda own, number: routed_block(jax.random.fold_in(arg_keys[10], 2), own, number, TOK_DEV, EXPERTS, 2, CAP, 2))(expert_ids_keys, expert_ids_turns).reshape((TOKENS, 2))
    grad_out = centred(arg_keys[11], (TOKENS, D), 0.25, 1.5, ((0, 256),))
    return dict(resid=resid, queries=queries, keys=keys, values=values, mod_scale=mod_scale, mod_shift=mod_shift, mod_gate=mod_gate, router=router, w_in=w_in, w_out=w_out, expert_ids=expert_ids, grad_out=grad_out)


NORM_EPSILON = 1e-06

def rounded(value):
    return lax.optimization_barrier(value.astype(jnp.bfloat16)).astype(jnp.float32)

def attend_clip(clip_item):
    query_clip, key_clip, value_clip = clip_item
    score_scale = 1.0 / math.sqrt(HDIM)
    query_heads = query_clip.astype(jnp.float32).reshape(CLIP, HEADS, HDIM)
    key_heads = key_clip.astype(jnp.float32).reshape(CLIP, HEADS, HDIM)
    value_heads = value_clip.astype(jnp.float32).reshape(CLIP, HEADS, HDIM)
    scores = jnp.einsum('qhd,khd->hqk', query_heads, key_heads) * score_scale
    row_top = lax.optimization_barrier(jnp.max(scores, axis=-1))
    exp_scores = jnp.exp(scores - row_top[..., None])
    row_total = lax.optimization_barrier(jnp.sum(exp_scores, axis=-1))
    mixed_values = jnp.einsum('hqk,khd->qhd', rounded(exp_scores), value_heads)
    attn = (mixed_values / row_total.T[:, :, None]).astype(jnp.bfloat16).reshape(CLIP, D)
    return (attn, row_top + jnp.log(row_total))

def attend_back(clip_item):
    query_clip, key_clip, value_clip, attn_clip, log_clip, grad_clip = clip_item
    score_scale = 1.0 / math.sqrt(HDIM)
    query_heads = query_clip.astype(jnp.float32).reshape(CLIP, HEADS, HDIM)
    key_heads = key_clip.astype(jnp.float32).reshape(CLIP, HEADS, HDIM)
    value_heads = value_clip.astype(jnp.float32).reshape(CLIP, HEADS, HDIM)
    attn_heads = attn_clip.astype(jnp.float32).reshape(CLIP, HEADS, HDIM)
    grad_heads = grad_clip.astype(jnp.float32).reshape(CLIP, HEADS, HDIM)
    scores = jnp.einsum('qhd,khd->hqk', query_heads, key_heads) * score_scale
    prob = jnp.exp(scores - log_clip[..., None])
    value_pull = jnp.einsum('qhd,khd->hqk', grad_heads, value_heads)
    row_dot = jnp.einsum('qhd,qhd->hq', grad_heads, attn_heads)
    score_grad = rounded(prob * (value_pull - row_dot[..., None]))
    grad_query = (jnp.einsum('hqk,khd->qhd', score_grad, key_heads) * score_scale).astype(jnp.bfloat16).reshape(CLIP, D)
    grad_blocks = score_grad.reshape(HEADS, N_CTX, TOK_DEV, CLIP)
    prob_blocks = rounded(prob).reshape(HEADS, N_CTX, TOK_DEV, CLIP)
    query_blocks = query_heads.reshape(N_CTX, TOK_DEV, HEADS, HDIM)
    grad_head_blocks = grad_heads.reshape(N_CTX, TOK_DEV, HEADS, HDIM)
    key_parts = rounded(jnp.einsum('hbqk,bqhd->bkhd', grad_blocks, query_blocks) * score_scale)
    value_parts = rounded(jnp.einsum('hbqk,bqhd->bkhd', prob_blocks, grad_head_blocks))
    grad_key = lax.optimization_barrier(jnp.sum(key_parts, axis=0)).astype(jnp.bfloat16).reshape(CLIP, D)
    grad_value = lax.optimization_barrier(jnp.sum(value_parts, axis=0)).astype(jnp.bfloat16).reshape(CLIP, D)
    return (grad_query, grad_key, grad_value)

def reference(resid, queries, keys, values, mod_scale, mod_shift, mod_gate, router, w_in, w_out, expert_ids, grad_out):
    query_clips = queries.reshape(CLIPS, CLIP, D)
    key_clips = keys.reshape(CLIPS, CLIP, D)
    value_clips = values.reshape(CLIPS, CLIP, D)
    attn, log_total = lax.map(attend_clip, (query_clips, key_clips, value_clips))
    hidden_sum = resid.astype(jnp.float32).reshape(CLIPS, CLIP, D) + attn.astype(jnp.float32)
    inv_rms = lax.rsqrt(lax.optimization_barrier(jnp.mean(hidden_sum * hidden_sum, axis=-1, keepdims=True)) + NORM_EPSILON)
    normed = hidden_sum * inv_rms
    lift_gain = 1.0 + mod_scale[:, None, :]
    normed_mod = (normed * lift_gain + mod_shift[:, None, :]).astype(jnp.bfloat16).reshape(TOKENS, D)
    logits = jnp.dot(normed_mod, router, preferred_element_type=jnp.float32)
    expert_range = jnp.arange(EXPERTS, dtype=jnp.int32)
    first_hot = (expert_ids[:, 0:1] == expert_range[None, :]).astype(jnp.float32)
    second_hot = (expert_ids[:, 1:2] == expert_range[None, :]).astype(jnp.float32)
    margin = lax.optimization_barrier(jnp.sum(logits * first_hot, axis=-1)) - lax.optimization_barrier(jnp.sum(logits * second_hot, axis=-1))
    gate_one = jax.nn.sigmoid(margin)
    gate_two = 1.0 - gate_one
    both_hot = (first_hot + second_hot).reshape(TOKENS // TOK_DEV, TOK_DEV, EXPERTS)
    earlier = (jnp.cumsum(both_hot, axis=1) - both_hot).reshape(TOKENS, EXPERTS)
    token_index = jnp.arange(TOKENS, dtype=jnp.int32)
    device_index = token_index // TOK_DEV
    place_one = device_index * CAP + lax.optimization_barrier(jnp.sum(earlier * first_hot, axis=-1)).astype(jnp.int32)
    place_two = device_index * CAP + lax.optimization_barrier(jnp.sum(earlier * second_hot, axis=-1)).astype(jnp.int32)
    rows_all = TOKENS // TOK_DEV * CAP
    slot_table = jnp.full((EXPERTS, rows_all), 2 * TOKENS, dtype=jnp.int32)
    slot_table = slot_table.at[expert_ids[:, 0], place_one].set(2 * token_index)
    slot_table = slot_table.at[expert_ids[:, 1], place_two].set(2 * token_index + 1)
    padded_in = jnp.concatenate([normed_mod, jnp.zeros((1, D), jnp.bfloat16)], axis=0)

    def expert_forward(expert_item):
        row_index, weight_in, weight_out = expert_item
        rows_in = padded_in[row_index // 2]
        pre_act = jnp.dot(rows_in, weight_in, preferred_element_type=jnp.float32)
        activated = jax.nn.gelu(pre_act).astype(jnp.bfloat16)
        blocks = jnp.einsum('rbf,bfd->brd', activated.astype(jnp.float32).reshape(rows_all, N_CTX, FF_BLOCK), weight_out.astype(jnp.float32).reshape(N_CTX, FF_BLOCK, D))
        return lax.optimization_barrier(jnp.sum(rounded(blocks), axis=0)).astype(jnp.bfloat16)
    expert_rows = lax.map(expert_forward, (slot_table, w_in, w_out))
    result_one = expert_rows[expert_ids[:, 0], place_one].astype(jnp.float32)
    result_two = expert_rows[expert_ids[:, 1], place_two].astype(jnp.float32)
    branch = gate_one[:, None] * result_one + gate_two[:, None] * result_two
    hidden_flat = hidden_sum.reshape(TOKENS, D)
    gated_branch = (mod_gate[:, None, :] * branch.reshape(CLIPS, CLIP, D)).reshape(TOKENS, D)
    mixed_out = (hidden_flat + gated_branch).astype(jnp.bfloat16)
    grad_float = grad_out.astype(jnp.float32)
    branch_grad = (mod_gate[:, None, :] * grad_float.reshape(CLIPS, CLIP, D)).reshape(TOKENS, D)
    grad_one = (gate_one[:, None] * branch_grad).astype(jnp.bfloat16)
    grad_two = (gate_two[:, None] * branch_grad).astype(jnp.bfloat16)
    gate_tilt = (lax.optimization_barrier(jnp.sum(branch_grad * result_one, axis=-1)) - lax.optimization_barrier(jnp.sum(branch_grad * result_two, axis=-1))) * gate_one * gate_two
    logit_grad = (gate_tilt[:, None] * (first_hot - second_hot)).astype(jnp.bfloat16)
    grad_router = jnp.dot(normed_mod.T, logit_grad, preferred_element_type=jnp.float32)
    back_router = jnp.dot(logit_grad, router.T, preferred_element_type=jnp.float32)
    pair_grads = jnp.stack([grad_one, grad_two], axis=1).reshape(2 * TOKENS, D)
    padded_grad = jnp.concatenate([pair_grads, jnp.zeros((1, D), jnp.bfloat16)], axis=0)

    def expert_backward(expert_item):
        row_index, weight_in, weight_out = expert_item
        rows_in = padded_in[row_index // 2]
        rows_grad = padded_grad[row_index]
        pre_act = jnp.dot(rows_in, weight_in, preferred_element_type=jnp.float32)
        activated = jax.nn.gelu(pre_act).astype(jnp.bfloat16)
        act_grad = jnp.dot(rows_grad, weight_out.T, preferred_element_type=jnp.float32)
        gelu_pull = jax.vjp(jax.nn.gelu, pre_act)[1]
        pre_grad = gelu_pull(act_grad)[0].astype(jnp.bfloat16)
        grad_in_weight = jnp.dot(rows_in.T, pre_grad, preferred_element_type=jnp.float32).astype(jnp.bfloat16)
        grad_out_weight = jnp.dot(activated.T, rows_grad, preferred_element_type=jnp.float32).astype(jnp.bfloat16)
        blocks = jnp.einsum('rbf,dbf->brd', pre_grad.astype(jnp.float32).reshape(rows_all, N_CTX, FF_BLOCK), weight_in.astype(jnp.float32).reshape(D, N_CTX, FF_BLOCK))
        return (lax.optimization_barrier(jnp.sum(rounded(blocks), axis=0)).astype(jnp.bfloat16), grad_in_weight, grad_out_weight)
    input_rows, grad_w_in, grad_w_out = lax.map(expert_backward, (slot_table, w_in, w_out))
    input_grad = input_rows[expert_ids[:, 0], place_one].astype(jnp.float32) + input_rows[expert_ids[:, 1], place_two].astype(jnp.float32) + back_router
    lifted = input_grad.reshape(CLIPS, CLIP, D) * lift_gain
    resid_grad = grad_float.reshape(CLIPS, CLIP, D) + inv_rms * (lifted - normed * lax.optimization_barrier(jnp.mean(lifted * normed, axis=-1, keepdims=True)))
    resid_grad = resid_grad.astype(jnp.bfloat16)
    grad_queries, grad_keys, grad_values = lax.map(attend_back, (query_clips, key_clips, value_clips, attn, log_total, resid_grad))
    return (mixed_out, resid_grad.reshape(TOKENS, D), grad_queries.reshape(TOKENS, D), grad_keys.reshape(TOKENS, D), grad_values.reshape(TOKENS, D), grad_w_in, grad_w_out, grad_router)
```

```python
import math

import jax
import jax.numpy as jnp
from jax import lax
from jax.experimental import pallas as pl
from jax.experimental.pallas import tpu as pltpu
from jax.sharding import PartitionSpec as P

D = 2048
HEADS = 16
HDIM = 128
EXPERTS = 64
TOK = 128
CTX = 4
CAP = 5
SLOTS = EXPERTS * CAP
CHUNKS = D // 128
WIDE = 512
FF_BLOCK = 256
PLAIN = CAP * CHUNKS
ROUTER_QUARTER = EXPERTS * CHUNKS // 4
TAGGED = PLAIN + 16
NORM_EPSILON = 1e-06
SCORE_SCALE = 1.0 / math.sqrt(HDIM)
GELU_C = math.sqrt(2.0 / math.pi)
BF = jnp.bfloat16
F32 = jnp.float32


def params(mib=44):
    return pltpu.CompilerParams(vmem_limit_bytes=mib << 20)


def dot(a, b):
    return jnp.dot(a, b, preferred_element_type=F32)


def dot_rows(a, b):
    return lax.dot_general(a, b, (((0,), (0,)), ((), ())), preferred_element_type=F32)


def dot_cols(a, b):
    return lax.dot_general(a, b, (((1,), (1,)), ((), ())), preferred_element_type=F32)


def shape(dims, kind):
    return jax.ShapeDtypeStruct(dims, kind)


def hbm(dims, kind):
    return pltpu.HBM(dims, kind)


def cost(micros):
    return pl.CostEstimate(flops=0, transcendentals=0, bytes_accessed=int(micros * 3e6))


SCALAR = pl.BlockSpec(memory_space=pltpu.SMEM)
IN_HBM = pl.BlockSpec(memory_space=pltpu.HBM)


def staged(body, scalars, args, out_shape, name, micros, scratch=(), unread=()):
    outs = out_shape if isinstance(out_shape, (list, tuple)) else [out_shape]
    front, read = len(scalars) + len(args), len(scalars) + len(args) + len(unread)

    def kernel(*refs):
        results = refs[read : read + len(outs)]
        own = refs[read + len(outs) : read + len(outs) + len(scratch)]
        buffers = refs[read + len(outs) + len(scratch) : -1]
        copies = [
            pltpu.make_async_copy(source, buffer, refs[-1].at[i])
            for i, (source, buffer) in enumerate(zip(refs[len(scalars) : front], buffers))
        ]
        for copy in copies:
            copy.start()
        for copy in copies:
            copy.wait()
        body(*refs[: len(scalars)], *buffers, *results, *own)

    return pl.pallas_call(
        kernel,
        in_specs=[SCALAR] * len(scalars) + [IN_HBM] * (len(args) + len(unread)),
        out_shape=out_shape,
        scratch_shapes=list(scratch)
        + [pltpu.VMEM(x.shape, x.dtype) for x in args]
        + [pltpu.SemaphoreType.DMA((len(args),))],
        compiler_params=params(),
        cost_estimate=cost(micros),
        name=name,
    )(*scalars, *args, *unread)


def to_blocks(rows, stage, block):
    for s in range(CAP):
        for c in range(CHUNKS):
            stage[pl.ds(s * CHUNKS + c, EXPERTS, stride=block), :] = rows[
                s * EXPERTS : (s + 1) * EXPERTS, c * 128 : (c + 1) * 128
            ]


def ref_to_blocks(rows, stage):
    @pl.loop(0, CAP)
    def _(s):
        for c in range(CHUNKS):
            stage[pl.ds(s * CHUNKS + c, EXPERTS, stride=PLAIN), :] = rows[
                pl.ds(pl.multiple_of(s * EXPERTS, EXPERTS), EXPERTS), c * 128 : (c + 1) * 128
            ]


def from_blocks(blocks, stage, rows, block):
    stage[...] = blocks.astype(F32).reshape(EXPERTS * block, 128)

    @pl.loop(0, CAP)
    def _(s):
        for c in range(CHUNKS):
            rows[pl.ds(pl.multiple_of(s * EXPERTS, EXPERTS), EXPERTS), c * 128 : (c + 1) * 128] = stage[
                pl.ds(s * CHUNKS + c, EXPERTS, stride=block), :
            ].astype(BF)


def one_hot(column, width):
    return (column == lax.broadcasted_iota(jnp.int32, (column.shape[0], width), 1)).astype(F32)


def group_cols(place, s):
    return pl.ds(pl.multiple_of(lax.rem(place[0] + s, CTX) * WIDE, WIDE), WIDE)


def pack_body(place, q, k, v, *outs):
    for s, out in enumerate(outs):
        cols = group_cols(place, s)
        out[0:TOK] = q[:, cols]
        out[TOK : 2 * TOK] = k[:, cols]
        out[2 * TOK :] = v[:, cols]


def pack(group, q, k, v):
    return staged(pack_body, [group], [q, k, v], [hbm((3 * TOK, WIDE), BF)] * CTX, "pack_heads", 3)


def unpack_body(place, *refs):
    dq, dk, dv = refs[CTX:]
    for s in range(CTX):
        x, cols = refs[s], group_cols(place, s)
        dq[:, cols] = x[0:TOK]
        dk[:, cols] = x[TOK : 2 * TOK]
        dv[:, cols] = x[2 * TOK :]


def unpack(group, parts):
    return staged(unpack_body, [group], parts, [hbm((TOK, D), BF)] * 3, "unpack_heads", 3)


def tagged_store(out, stage, tag_rows):
    out[:, 0:PLAIN, :] = stage[...].reshape(EXPERTS, PLAIN, 128).astype(BF)
    row = lax.broadcasted_iota(jnp.int32, (EXPERTS, 16, 128), 1)
    tags = jnp.zeros((EXPERTS, 16, 128), F32)
    for i, tag in enumerate(tag_rows):
        tags = jnp.where(row == i, tag[:, None, :], tags)
    out[:, PLAIN:, :] = tags.astype(BF)


def slots_to_lanes(columns):
    lane = lax.broadcasted_iota(jnp.int32, (EXPERTS, 128), 1)
    table = jnp.zeros((EXPERTS, 128), F32)
    for s in range(CAP):
        table = jnp.where(lane == s, columns[s * EXPERTS : (s + 1) * EXPERTS], table)
    return table


def grads_body(grad_out, mod_gate, ids, place_out, send, stage):
    first, second = ids[:, 0:1], ids[:, 1:2]
    first_hot, second_hot = one_hot(first, EXPERTS), one_hot(second, EXPERTS)
    both = first_hot + second_hot
    rows = lax.broadcasted_iota(jnp.int32, (TOK, TOK), 0)
    cols = lax.broadcasted_iota(jnp.int32, (TOK, TOK), 1)
    earlier = dot((cols < rows).astype(BF), both.astype(BF))
    pos_one = jnp.sum(earlier * first_hot, axis=1, keepdims=True).astype(jnp.int32)
    pos_two = jnp.sum(earlier * second_hot, axis=1, keepdims=True).astype(jnp.int32)
    place_one = pos_one * EXPERTS + first
    place_two = pos_two * EXPERTS + second
    lane = lax.broadcasted_iota(jnp.int32, (TOK, 2), 1)
    place_out[...] = jnp.where(lane == 0, place_one, place_two)
    pick_one = one_hot(place_one, SLOTS).astype(BF)
    pick_two = one_hot(place_two, SLOTS).astype(BF)
    branch_grad = (mod_gate[...] * grad_out[...].astype(F32)).astype(BF)
    to_blocks(dot_rows(pick_one + pick_two, branch_grad), stage, PLAIN)
    other_one = jnp.broadcast_to(second.astype(F32), (TOK, 128)).astype(BF)
    other_two = jnp.broadcast_to(first.astype(F32), (TOK, 128)).astype(BF)
    partner = dot_rows(pick_one, other_one) + dot_rows(pick_two, other_two)
    tagged_store(send, stage, [slots_to_lanes(partner)])


def send_grads(grad_out, mod_gate, ids, after):
    return staged(
        grads_body,
        [],
        [grad_out, mod_gate, ids],
        [hbm((TOK, 2), jnp.int32), hbm((EXPERTS, TAGGED, 128), BF)],
        "dispatch_grads",
        3,
        scratch=[pltpu.VMEM((EXPERTS * PLAIN, 128), F32)],
        unread=[after],
    )


def heads_of(parts, which):
    return jnp.concatenate([x[which * TOK : (which + 1) * TOK, :] for x in parts], axis=0)


def attend_body(*refs):
    parts, outs = refs[:CTX], refs[CTX:]
    q, k, v = heads_of(parts, 0), heads_of(parts, 1), heads_of(parts, 2)
    scores = dot_cols(q, k) * SCORE_SCALE
    top = jnp.max(scores, axis=1, keepdims=True)
    weights = jnp.exp(scores - top)
    total = jnp.sum(weights, axis=1, keepdims=True)
    mixed = (dot(weights.astype(BF), v) / total).astype(BF)
    for s, out in enumerate(outs):
        out[...] = mixed[s * TOK : (s + 1) * TOK]


ONE_HEAD = pl.BlockSpec((TOK, HDIM), lambda h: (0, h))
THREE_HEADS = pl.BlockSpec((3 * TOK, HDIM), lambda h: (0, h))


def attend(parts):
    return pl.pallas_call(
        attend_body,
        grid=(WIDE // HDIM,),
        in_specs=[THREE_HEADS] * CTX,
        out_specs=[ONE_HEAD] * CTX,
        out_shape=[hbm((TOK, WIDE), BF)] * CTX,
        compiler_params=params(),
        cost_estimate=cost(10),
        name="attend_forward",
    )(*parts)


def attend_back_body(*refs):
    parts, attn, grads, outs = refs[:CTX], refs[CTX : 2 * CTX], refs[2 * CTX : 3 * CTX], refs[3 * CTX :]
    q, k, v = heads_of(parts, 0), heads_of(parts, 1), heads_of(parts, 2)
    o, g = heads_of(attn, 0), heads_of(grads, 0)
    scores = dot_cols(q, k) * SCORE_SCALE
    top = jnp.max(scores, axis=1, keepdims=True)
    total = jnp.sum(jnp.exp(scores - top), axis=1, keepdims=True)
    prob = jnp.exp(scores - (top + jnp.log(total)))
    row_dot = jnp.sum(g.astype(F32) * o.astype(F32), axis=1, keepdims=True)
    score_grad = (prob * (dot_cols(g, v) - row_dot)).astype(BF)
    dq = (dot(score_grad, k) * SCORE_SCALE).astype(BF)
    dk = (dot_rows(score_grad, q) * SCORE_SCALE).astype(BF)
    dv = dot_rows(prob.astype(BF), g).astype(BF)
    for s, out in enumerate(outs):
        rows = slice(s * TOK, (s + 1) * TOK)
        out[0:TOK] = dq[rows]
        out[TOK : 2 * TOK] = dk[rows]
        out[2 * TOK :] = dv[rows]


def attend_back(parts, attn, grads):
    return pl.pallas_call(
        attend_back_body,
        grid=(WIDE // HDIM,),
        in_specs=[THREE_HEADS] * CTX + [ONE_HEAD] * (2 * CTX),
        out_specs=[THREE_HEADS] * CTX,
        out_shape=[hbm((3 * TOK, WIDE), BF)] * CTX,
        compiler_params=params(),
        cost_estimate=cost(100),
        name="attend_backward",
    )(*parts, *attn, *grads)


def norm_body(
    group, attn_0, attn_1, attn_2, attn_3, resid, scale, shift, router, ids, place,
    send, kept, gate, inverse, hidden, stage,
):
    square = jnp.zeros((TOK, 1), F32)
    for s, attn in enumerate((attn_0, attn_1, attn_2, attn_3)):
        cols = group_cols(group, s)
        part = resid[:, cols].astype(F32) + attn[...].astype(F32)
        hidden[:, cols] = part
        square = square + jnp.sum(part * part, axis=1, keepdims=True)
    inv = lax.rsqrt(square / D + NORM_EPSILON)
    normed_mod = (hidden[...] * inv * (1.0 + scale[...]) + shift[...]).astype(BF)
    kept[...] = normed_mod
    inverse[...] = jnp.broadcast_to(inv, (TOK, 128))
    pick = (one_hot(place[:, 0:1], SLOTS) + one_hot(place[:, 1:2], SLOTS)).astype(BF)
    to_blocks(dot_rows(pick, normed_mod), stage, PLAIN)
    send[...] = stage[...].reshape(EXPERTS, PLAIN, 128).astype(BF)
    logits = dot_cols(normed_mod, router[...])
    hot = one_hot(ids[:, 0:1], EXPERTS) - one_hot(ids[:, 1:2], EXPERTS)
    margin = jnp.sum(logits * hot, axis=1, keepdims=True)
    gate[...] = jnp.broadcast_to(jax.nn.sigmoid(margin), (TOK, 128))


def send_rows(group, attn, resid, scale, shift, router, ids, place):
    return staged(
        norm_body,
        [group],
        [*attn, resid, scale, shift, router, ids, place],
        [
            hbm((EXPERTS, PLAIN, 128), BF),
            hbm((TOK, D), BF),
            hbm((TOK, 128), F32),
            hbm((TOK, 128), F32),
        ],
        "norm_dispatch",
        3,
        scratch=[pltpu.VMEM((TOK, D), F32), pltpu.VMEM((EXPERTS * PLAIN, 128), F32)],
    )


def gelu_terms(pre):
    square = pre * pre
    turn = jnp.tanh(GELU_C * (pre + 0.044715 * pre * square))
    return square, turn


def forward_body(
    arrived, arrived_grads, w_in, w_out, router, own,
    rows, row_grads, pre_out, y_send, pull_send,
    stage, y_sum, branch_grad,
):
    step = pl.program_id(0)

    @pl.when(step == 0)
    def _():
        from_blocks(arrived_grads[:, 0:PLAIN, :], stage, branch_grad, PLAIN)
        from_blocks(arrived[...], stage, rows, PLAIN)
        partner_table = arrived_grads[:, PLAIN : PLAIN + 16, :].astype(F32)[:, 0, :]
        partner = jnp.concatenate(
            [partner_table[:, s : s + 1] for s in range(CAP)], axis=0
        ).astype(jnp.int32)
        logits = dot_cols(rows[...], router[...])
        margin = jnp.sum(logits * (own[...] - one_hot(partner, EXPERTS)), axis=1, keepdims=True)
        row_grads[...] = (jax.nn.sigmoid(margin) * branch_grad[...].astype(F32)).astype(BF)
        y_sum[...] = jnp.zeros_like(y_sum)

    pre = dot(rows[...], w_in[0])
    pre_out[0] = pre
    _, turn = gelu_terms(pre)
    act = (0.5 * pre * (1.0 + turn)).astype(BF)
    y_sum[...] += dot(act, w_out[0]).astype(BF).astype(F32)

    @pl.when(step == CTX - 1)
    def _():
        pull = jnp.sum(
            branch_grad[...].astype(F32) * y_sum[...].astype(BF).astype(F32), axis=1, keepdims=True
        )
        pull_send[...] = jnp.broadcast_to(slots_to_lanes(pull)[:, None, :], (EXPERTS, 8, 128))
        ref_to_blocks(y_sum, stage)
        y_send[...] = stage[...].reshape(EXPERTS, PLAIN, 128).astype(BF)


def whole(*dims):
    return pl.BlockSpec(dims, lambda b: (0,) * len(dims))


def of_block(*dims):
    return pl.BlockSpec((1,) + dims, lambda b: (b,) + (0,) * len(dims))


def experts_forward(arrived, arrived_grads, w_in, w_out, router, own):
    return pl.pallas_call(
        forward_body,
        grid=(CTX,),
        in_specs=[
            whole(EXPERTS, PLAIN, 128),
            whole(EXPERTS, TAGGED, 128),
            of_block(D, FF_BLOCK),
            of_block(FF_BLOCK, D),
            whole(EXPERTS, D),
            whole(1, EXPERTS),
        ],
        out_specs=[
            whole(SLOTS, D),
            whole(SLOTS, D),
            of_block(SLOTS, FF_BLOCK),
            whole(EXPERTS, PLAIN, 128),
            whole(EXPERTS, 8, 128),
        ],
        out_shape=[
            hbm((SLOTS, D), BF),
            hbm((SLOTS, D), BF),
            hbm((CTX, SLOTS, FF_BLOCK), F32),
            hbm((EXPERTS, PLAIN, 128), BF),
            hbm((EXPERTS, 8, 128), F32),
        ],
        scratch_shapes=[
            pltpu.VMEM((EXPERTS * PLAIN, 128), F32),
            pltpu.VMEM((SLOTS, D), F32),
            pltpu.VMEM((SLOTS, D), BF),
        ],
        compiler_params=params(),
        cost_estimate=cost(10),
        name="expert_forward",
    )(arrived, arrived_grads, w_in, w_out, router, own)


def backward_body(rows, row_grads, pre_in, w_in, w_out, in_send, out_send, part_send, stage, part_sum):
    step = pl.program_id(0)

    @pl.when(step == 0)
    def _():
        part_sum[...] = jnp.zeros_like(part_sum)

    pre = pre_in[0]
    square, turn = gelu_terms(pre)
    act = (0.5 * pre * (1.0 + turn)).astype(BF)
    slope = 0.5 * (1.0 + turn) + 0.5 * pre * (1.0 - turn * turn) * (
        GELU_C * (1.0 + 3.0 * 0.044715 * square)
    )
    pre_grad = (dot_cols(row_grads[...], w_out[0]) * slope).astype(BF)
    part_sum[...] += dot_cols(pre_grad, w_in[0]).astype(BF).astype(F32)
    in_send[0] = dot_rows(rows[...], pre_grad).astype(BF)
    out_send[0] = dot_rows(act, row_grads[...]).astype(BF)

    @pl.when(step == CTX - 1)
    def _():
        ref_to_blocks(part_sum, stage)
        part_send[...] = stage[...].reshape(EXPERTS, PLAIN, 128).astype(BF)


def experts_backward(rows, row_grads, pre, w_in, w_out):
    return pl.pallas_call(
        backward_body,
        grid=(CTX,),
        in_specs=[
            whole(SLOTS, D),
            whole(SLOTS, D),
            of_block(SLOTS, FF_BLOCK),
            of_block(D, FF_BLOCK),
            of_block(FF_BLOCK, D),
        ],
        out_specs=[of_block(D, FF_BLOCK), of_block(FF_BLOCK, D), whole(EXPERTS, PLAIN, 128)],
        out_shape=[
            hbm((CTX, D, FF_BLOCK), BF),
            hbm((CTX, FF_BLOCK, D), BF),
            hbm((EXPERTS, PLAIN, 128), BF),
        ],
        scratch_shapes=[pltpu.VMEM((EXPERTS * PLAIN, 128), F32), pltpu.VMEM((SLOTS, D), F32)],
        compiler_params=params(),
        cost_estimate=cost(15),
        name="expert_backward",
    )(rows, row_grads, pre, w_in, w_out)


def one_hots(ids):
    return one_hot(ids[:, 0:1], EXPERTS), one_hot(ids[:, 1:2], EXPERTS)


def lane_pull(hot, table, lane_hot):
    taken = jnp.zeros((TOK, 128), F32)
    for _ in range(3):
        part = table.astype(BF)
        taken = taken + dot(hot.astype(BF), part)
        table = table - part.astype(F32)
    return jnp.sum(taken * lane_hot, axis=1, keepdims=True)


def tilt_body(own, arrived, kept, gate, ids, place, logit_out, router_0, router_1, router_2, router_3, twice):
    first_hot, second_hot = one_hots(ids)
    table = arrived[:, 0, :]
    lane_one = one_hot(lax.shift_right_logical(place[:, 0:1], 6), 128)
    lane_two = one_hot(lax.shift_right_logical(place[:, 1:2], 6), 128)
    pull_one = lane_pull(first_hot, table, lane_one)
    pull_two = lane_pull(second_hot, table, lane_two)
    gate_one = gate[:, 0:1]
    tilt = (pull_one - pull_two) * gate_one * (1.0 - gate_one)
    logit_grad = (tilt * (first_hot - second_hot)).astype(BF)
    logit_out[...] = logit_grad
    terms = dot_rows(logit_grad, kept[...])
    for c in range(CHUNKS):
        chunk = terms[:, c * 128 : (c + 1) * 128]
        twice[pl.ds(c, EXPERTS, stride=CHUNKS), :] = chunk
        twice[pl.ds(EXPERTS * CHUNKS + c, EXPERTS, stride=CHUNKS), :] = chunk
    for k, send in enumerate((router_0, router_1, router_2, router_3)):
        first = pl.multiple_of(own[0] * CHUNKS, CHUNKS) + k * ROUTER_QUARTER
        send[...] = twice[pl.ds(first, ROUTER_QUARTER), :]


def router_terms_of(own, arrived, kept, gate, ids, place):
    return staged(
        tilt_body,
        [own],
        [arrived, kept, gate, ids, place],
        [hbm((TOK, EXPERTS), BF)] + [hbm((ROUTER_QUARTER, 128), F32)] * 4,
        "router_terms",
        3,
        scratch=[pltpu.VMEM((2 * EXPERTS * CHUNKS, 128), F32)],
    )


def resid_body(
    group, arrived, attn_0, attn_1, attn_2, attn_3, resid, grad_out, scale, router, place, logit_grad, inverse,
    resid_grad, send_0, send_1, send_2, send_3,
    stage, back, normed, lifted,
):
    from_blocks(arrived[...], stage, back, PLAIN)
    pick = (one_hot(place[:, 0:1], SLOTS) + one_hot(place[:, 1:2], SLOTS)).astype(BF)
    input_grad = dot(pick, back[...]) + dot(logit_grad[...], router[...])
    inv = inverse[:, 0:1]
    lifted[...] = input_grad * (1.0 + scale[...])
    mean = jnp.zeros((TOK, 1), F32)
    for s, attn in enumerate((attn_0, attn_1, attn_2, attn_3)):
        cols = group_cols(group, s)
        part = (resid[:, cols].astype(F32) + attn[...].astype(F32)) * inv
        normed[:, cols] = part
        mean = mean + jnp.sum(part * lifted[:, cols], axis=1, keepdims=True)
    mean = mean / D
    for s, send in enumerate((send_0, send_1, send_2, send_3)):
        cols = group_cols(group, s)
        part = grad_out[:, cols].astype(F32) + inv * (lifted[:, cols] - normed[:, cols] * mean)
        low_part = part.astype(BF)
        resid_grad[:, cols] = low_part
        send[...] = low_part


def resid_back(group, arrived, attn, resid, grad_out, scale, router, place, logit_grad, inverse, after):
    return staged(
        resid_body,
        [group],
        [arrived, *attn, resid, grad_out, scale, router, place, logit_grad, inverse],
        [hbm((TOK, D), BF)] + [hbm((TOK, WIDE), BF)] * CTX,
        "resid_backward",
        30,
        scratch=[
            pltpu.VMEM((EXPERTS * PLAIN, 128), F32),
            pltpu.VMEM((SLOTS, D), BF),
            pltpu.VMEM((TOK, D), F32),
            pltpu.VMEM((TOK, D), F32),
        ],
        unread=[after],
    )


def mixed_body(group, arrived, attn_0, attn_1, attn_2, attn_3, resid, mod_gate, place, gate, out, stage, back, branch):
    from_blocks(arrived[...], stage, back, PLAIN)
    gate_one = gate[:, 0:1]
    result_one = dot(one_hot(place[:, 0:1], SLOTS).astype(BF), back[...])
    result_two = dot(one_hot(place[:, 1:2], SLOTS).astype(BF), back[...])
    branch[...] = mod_gate[...] * (gate_one * result_one + (1.0 - gate_one) * result_two)
    for s, attn in enumerate((attn_0, attn_1, attn_2, attn_3)):
        cols = group_cols(group, s)
        hidden = resid[:, cols].astype(F32) + attn[...].astype(F32)
        out[:, cols] = (hidden + branch[:, cols]).astype(BF)


def mix(group, arrived, attn, resid, mod_gate, place, gate):
    return staged(
        mixed_body,
        [group],
        [arrived, *attn, resid, mod_gate, place, gate],
        hbm((TOK, D), BF),
        "mixed_output",
        4,
        scratch=[
            pltpu.VMEM((EXPERTS * PLAIN, 128), F32),
            pltpu.VMEM((SLOTS, D), BF),
            pltpu.VMEM((TOK, D), F32),
        ],
    )


def router_body(own, part_0, part_1, part_2, part_3, out, twice):
    quarter = EXPERTS * CHUNKS // 4
    for i, part in enumerate((part_0, part_1, part_2, part_3)):
        twice[i * quarter : (i + 1) * quarter] = part[...]
        twice[(i + 4) * quarter : (i + 5) * quarter] = part[...]
    first = (EXPERTS - own[0]) * CHUNKS
    for c in range(CHUNKS):
        out[:, c * 128 : (c + 1) * 128] = twice[pl.ds(first + c, EXPERTS, stride=CHUNKS), :]


def add_four_body(*refs):
    total = refs[0][...] + refs[1][...] + refs[2][...] + refs[3][...]
    outs = refs[4:]
    rows = total.shape[0] // len(outs)
    for i, out in enumerate(outs):
        out[...] = total[i * rows : (i + 1) * rows]


def add_four(parts, pieces, after=()):
    rows = parts[0].shape[0] // pieces
    outs = [hbm((rows, 128), F32)] * pieces
    return staged(add_four_body, [], parts, outs, "add_four", 1, unread=after)


def order_router(own, parts):
    return staged(
        router_body,
        [own],
        parts,
        hbm((EXPERTS, D), F32),
        "order_router",
        2,
        scratch=[pltpu.VMEM((2 * EXPERTS * CHUNKS, 128), F32)],
    )


def swap(x):
    return lax.all_to_all(x, "expert", split_axis=0, concat_axis=0, tiled=True)


def shift(x, axis, count, step):
    return lax.ppermute(x, axis, [(i, (i + step) % count) for i in range(count)])


def around(parts, sign):
    return [parts[0]] + [shift(parts[s], "ctx", CTX, sign * s) for s in range(1, CTX)]


def spread(parts, digit):
    return [parts[0]] + [shift(parts[k], "expert", EXPERTS, k * digit) for k in range(1, 4)]


def local(
    resid, queries, keys, values, mod_scale, mod_shift, mod_gate, router, w_in, w_out, expert_ids, grad_out
):
    group = lax.axis_index("ctx").astype(jnp.int32)[None]
    expert = lax.axis_index("expert").astype(jnp.int32)
    own = (jnp.arange(EXPERTS, dtype=jnp.int32) == expert).astype(F32)[None, :]
    router_rows = router.T
    packed = pack(group, queries, keys, values)
    heads = around(packed, 1)
    place, grads = send_grads(grad_out, mod_gate, expert_ids, packed[0])
    arrived_grads = swap(grads)
    full_in = lax.all_gather(w_in, "ctx", axis=0, tiled=True)
    full_out = lax.all_gather(w_out, "ctx", axis=0, tiled=True)
    attn_heads = attend(heads)
    attn = around(attn_heads, -1)
    rows, kept, gate, inverse = send_rows(
        group, attn, resid, mod_scale, mod_shift, router_rows, expert_ids, place
    )
    arrived = swap(rows)
    flat_rows, flat_grads, pre_act, y_rows, pulls = experts_forward(
        arrived, arrived_grads, full_in, full_out, router_rows, own
    )
    pulls = swap(pulls)
    in_terms, out_terms, part_rows = experts_backward(flat_rows, flat_grads, pre_act, full_in, full_out)
    parts = swap(part_rows)
    logit_grad, *router_terms = router_terms_of(expert[None], pulls, kept, gate, expert_ids, place)
    in_terms, out_terms, _ = lax.optimization_barrier((in_terms, out_terms, logit_grad))
    grad_w_in, grad_w_out = (
        lax.psum_scatter(x, "ctx", scatter_dimension=0, tiled=True) for x in (in_terms, out_terms)
    )
    for digit in (16, 4, 1):
        router_terms = add_four(spread(router_terms, digit), 4 if digit > 1 else 1)
    resid_grad, *head_grads = resid_back(
        group, parts, attn, resid, grad_out, mod_scale, router_rows, place, logit_grad, inverse,
        router_terms[0],
    )
    attn_grads = around(head_grads, 1)
    late_rows, _ = lax.optimization_barrier((y_rows, head_grads[0]))
    outputs = swap(late_rows)
    head_terms = attend_back(heads, attn_heads, attn_grads)
    head_sums = around(head_terms, -1)
    pieces = router_terms[0]
    pieces = add_four(around([pieces] * CTX, 1), 1, [head_terms[0]])[0]
    for digit in (1, 4, 16):
        quarters = spread([pieces] * 4, -digit)
        pieces = jnp.concatenate(quarters, axis=0)
    grad_router = order_router(expert[None], quarters).T
    grad_queries, grad_keys, grad_values = unpack(group, head_sums)
    mixed_out = mix(group, outputs, attn, resid, mod_gate, place, gate)
    return (
        mixed_out,
        resid_grad,
        grad_queries,
        grad_keys,
        grad_values,
        grad_w_in,
        grad_w_out,
        grad_router,
    )


def solution(mesh):
    tokens = P(("expert", "ctx"), None)
    clip = P("expert", None)
    return jax.shard_map(
        local,
        mesh=mesh,
        in_specs=(
            tokens, tokens, tokens, tokens, clip, clip, clip, P(),
            P("expert", None, "ctx"), P("expert", "ctx", None), tokens, tokens,
        ),
        out_specs=(
            tokens, tokens, tokens, tokens, tokens,
            P("expert", None, "ctx"), P("expert", "ctx", None), P(),
        ),
        check_vma=False,
    )
```

```python
import math

import jax
import jax.numpy as jnp
from jax import lax
from jax.experimental import pallas as pl
from jax.experimental.pallas import tpu as pltpu
from jax.sharding import PartitionSpec as P

D = 2048
HEADS = 16
HDIM = 128
EXPERTS = 64
TOK = 128
CTX = 4
CAP = 5
SLOTS = EXPERTS * CAP
CHUNKS = D // 128
WIDE = 512
FF_BLOCK = 256
PLAIN = CAP * CHUNKS
ROUTER_QUARTER = EXPERTS * CHUNKS // 4
TAGGED = PLAIN + 16
NORM_EPSILON = 1e-06
SCORE_SCALE = 1.0 / math.sqrt(HDIM)
GELU_C = math.sqrt(2.0 / math.pi)
BF = jnp.bfloat16
F32 = jnp.float32


def params(mib=44):
    return pltpu.CompilerParams(vmem_limit_bytes=mib << 20)


def dot(a, b):
    return jnp.dot(a, b, preferred_element_type=F32)


def dot_rows(a, b):
    return lax.dot_general(a, b, (((0,), (0,)), ((), ())), preferred_element_type=F32)


def dot_cols(a, b):
    return lax.dot_general(a, b, (((1,), (1,)), ((), ())), preferred_element_type=F32)


def shape(dims, kind):
    return jax.ShapeDtypeStruct(dims, kind)


def hbm(dims, kind):
    return pltpu.HBM(dims, kind)


def cost(micros):
    return pl.CostEstimate(flops=0, transcendentals=0, bytes_accessed=int(micros * 3e6))


SCALAR = pl.BlockSpec(memory_space=pltpu.SMEM)
IN_HBM = pl.BlockSpec(memory_space=pltpu.HBM)


def staged(body, scalars, args, out_shape, name, micros, scratch=(), unread=(), mib=44):
    outs = out_shape if isinstance(out_shape, (list, tuple)) else [out_shape]
    front, read = len(scalars) + len(args), len(scalars) + len(args) + len(unread)

    def kernel(*refs):
        results = refs[read : read + len(outs)]
        own = refs[read + len(outs) : read + len(outs) + len(scratch)]
        buffers = refs[read + len(outs) + len(scratch) : -1]
        copies = [
            pltpu.make_async_copy(source, buffer, refs[-1].at[i])
            for i, (source, buffer) in enumerate(zip(refs[len(scalars) : front], buffers))
        ]
        for copy in copies:
            copy.start()
        for copy in copies:
            copy.wait()
        body(*refs[: len(scalars)], *buffers, *results, *own)

    return pl.pallas_call(
        kernel,
        in_specs=[SCALAR] * len(scalars) + [IN_HBM] * (len(args) + len(unread)),
        out_shape=out_shape,
        scratch_shapes=list(scratch)
        + [pltpu.VMEM(x.shape, x.dtype) for x in args]
        + [pltpu.SemaphoreType.DMA((len(args),))],
        compiler_params=params(mib),
        cost_estimate=cost(micros),
        name=name,
    )(*scalars, *args, *unread)


def to_blocks(rows, stage, block):
    for s in range(CAP):
        for c in range(CHUNKS):
            stage[pl.ds(s * CHUNKS + c, EXPERTS, stride=block), :] = rows[
                s * EXPERTS : (s + 1) * EXPERTS, c * 128 : (c + 1) * 128
            ]


def ref_to_blocks(rows, stage):
    @pl.loop(0, CAP)
    def _(s):
        for c in range(CHUNKS):
            stage[pl.ds(s * CHUNKS + c, EXPERTS, stride=PLAIN), :] = rows[
                pl.ds(pl.multiple_of(s * EXPERTS, EXPERTS), EXPERTS), c * 128 : (c + 1) * 128
            ]


def from_blocks(blocks, stage, rows, block):
    stage[...] = blocks.astype(F32).reshape(EXPERTS * block, 128)

    @pl.loop(0, CAP)
    def _(s):
        for c in range(CHUNKS):
            rows[pl.ds(pl.multiple_of(s * EXPERTS, EXPERTS), EXPERTS), c * 128 : (c + 1) * 128] = stage[
                pl.ds(s * CHUNKS + c, EXPERTS, stride=block), :
            ].astype(BF)


def one_hot(column, width):
    return (column == lax.broadcasted_iota(jnp.int32, (column.shape[0], width), 1)).astype(F32)


def group_cols(place, s):
    return pl.ds(pl.multiple_of(lax.rem(place[0] + s, CTX) * WIDE, WIDE), WIDE)


def pack_body(place, q, k, v, *outs):
    for s, out in enumerate(outs):
        cols = group_cols(place, s)
        out[0:TOK] = q[:, cols]
        out[TOK : 2 * TOK] = k[:, cols]
        out[2 * TOK :] = v[:, cols]


def pack(group, q, k, v):
    return staged(pack_body, [group], [q, k, v], [hbm((3 * TOK, WIDE), BF)] * CTX, "pack_heads", 3)


def unpack_body(place, *refs):
    dq, dk, dv = refs[CTX:]
    for s in range(CTX):
        x, cols = refs[s], group_cols(place, s)
        dq[:, cols] = x[0:TOK]
        dk[:, cols] = x[TOK : 2 * TOK]
        dv[:, cols] = x[2 * TOK :]


def unpack(group, parts):
    return staged(unpack_body, [group], parts, [hbm((TOK, D), BF)] * 3, "unpack_heads", 60)


def tagged_store(out, stage, tag_rows):
    out[:, 0:PLAIN, :] = stage[...].reshape(EXPERTS, PLAIN, 128).astype(BF)
    row = lax.broadcasted_iota(jnp.int32, (EXPERTS, 16, 128), 1)
    tags = jnp.zeros((EXPERTS, 16, 128), F32)
    for i, tag in enumerate(tag_rows):
        tags = jnp.where(row == i, tag[:, None, :], tags)
    out[:, PLAIN:, :] = tags.astype(BF)


def slots_to_lanes(columns):
    lane = lax.broadcasted_iota(jnp.int32, (EXPERTS, 128), 1)
    table = jnp.zeros((EXPERTS, 128), F32)
    for s in range(CAP):
        table = jnp.where(lane == s, columns[s * EXPERTS : (s + 1) * EXPERTS], table)
    return table


def grads_body(grad_out, mod_gate, ids, place_out, send, stage):
    first, second = ids[:, 0:1], ids[:, 1:2]
    first_hot, second_hot = one_hot(first, EXPERTS), one_hot(second, EXPERTS)
    both = first_hot + second_hot
    rows = lax.broadcasted_iota(jnp.int32, (TOK, TOK), 0)
    cols = lax.broadcasted_iota(jnp.int32, (TOK, TOK), 1)
    earlier = dot((cols < rows).astype(BF), both.astype(BF))
    pos_one = jnp.sum(earlier * first_hot, axis=1, keepdims=True).astype(jnp.int32)
    pos_two = jnp.sum(earlier * second_hot, axis=1, keepdims=True).astype(jnp.int32)
    place_one = pos_one * EXPERTS + first
    place_two = pos_two * EXPERTS + second
    lane = lax.broadcasted_iota(jnp.int32, (TOK, 2), 1)
    place_out[...] = jnp.where(lane == 0, place_one, place_two)
    pick_one = one_hot(place_one, SLOTS).astype(BF)
    pick_two = one_hot(place_two, SLOTS).astype(BF)
    branch_grad = (mod_gate[...] * grad_out[...].astype(F32)).astype(BF)
    to_blocks(dot_rows(pick_one + pick_two, branch_grad), stage, PLAIN)
    other_one = jnp.broadcast_to(second.astype(F32), (TOK, 128)).astype(BF)
    other_two = jnp.broadcast_to(first.astype(F32), (TOK, 128)).astype(BF)
    partner = dot_rows(pick_one, other_one) + dot_rows(pick_two, other_two)
    tagged_store(send, stage, [slots_to_lanes(partner)])


def send_grads(grad_out, mod_gate, ids, after):
    return staged(
        grads_body,
        [],
        [grad_out, mod_gate, ids],
        [hbm((TOK, 2), jnp.int32), hbm((EXPERTS, TAGGED, 128), BF)],
        "dispatch_grads",
        3,
        scratch=[pltpu.VMEM((EXPERTS * PLAIN, 128), F32)],
        unread=[after],
    )


def heads_of(parts, which):
    return jnp.concatenate([x[which * TOK : (which + 1) * TOK, :] for x in parts], axis=0)


def attend_body(*refs):
    parts, outs, saved = refs[:CTX], refs[CTX : 2 * CTX], refs[2 * CTX]
    q, k, v = heads_of(parts, 0), heads_of(parts, 1), heads_of(parts, 2)
    scores = dot_cols(q, k) * SCORE_SCALE
    top = jnp.max(scores, axis=1, keepdims=True)
    weights = jnp.exp(scores - top)
    total = jnp.sum(weights, axis=1, keepdims=True)
    mixed = (dot(weights.astype(BF), v) / total).astype(BF)
    for i, x in enumerate((q, k, v, mixed)):
        saved[i] = x
    for s, out in enumerate(outs):
        out[...] = mixed[s * TOK : (s + 1) * TOK]


ONE_HEAD = pl.BlockSpec((TOK, HDIM), lambda h: (0, h))
THREE_HEADS = pl.BlockSpec((3 * TOK, HDIM), lambda h: (0, h))
SAVED = pl.BlockSpec((4, CTX * TOK, HDIM), lambda h: (0, 0, h))


def attend(parts):
    return pl.pallas_call(
        attend_body,
        grid=(WIDE // HDIM,),
        in_specs=[THREE_HEADS] * CTX,
        out_specs=[ONE_HEAD] * CTX + [SAVED],
        out_shape=[hbm((TOK, WIDE), BF)] * CTX + [hbm((4, CTX * TOK, WIDE), BF)],
        compiler_params=params(),
        cost_estimate=cost(10),
        name="attend_forward",
    )(*parts)


def attend_back_body(saved, *refs):
    grads, outs = refs[:CTX], refs[CTX:]
    q, k, v, o = (saved[i] for i in range(4))
    g = heads_of(grads, 0)
    scores = dot_cols(q, k) * SCORE_SCALE
    top = jnp.max(scores, axis=1, keepdims=True)
    total = jnp.sum(jnp.exp(scores - top), axis=1, keepdims=True)
    prob = jnp.exp(scores - (top + jnp.log(total)))
    row_dot = jnp.sum(g.astype(F32) * o.astype(F32), axis=1, keepdims=True)
    score_grad = (prob * (dot_cols(g, v) - row_dot)).astype(BF)
    dq = (dot(score_grad, k) * SCORE_SCALE).astype(BF)
    dk = (dot_rows(score_grad, q) * SCORE_SCALE).astype(BF)
    dv = dot_rows(prob.astype(BF), g).astype(BF)
    for s, out in enumerate(outs):
        rows = slice(s * TOK, (s + 1) * TOK)
        out[0:TOK] = dq[rows]
        out[TOK : 2 * TOK] = dk[rows]
        out[2 * TOK :] = dv[rows]


def attend_back(saved, grads):
    return pl.pallas_call(
        attend_back_body,
        grid=(WIDE // HDIM,),
        in_specs=[SAVED] + [ONE_HEAD] * CTX,
        out_specs=[THREE_HEADS] * CTX,
        out_shape=[hbm((3 * TOK, WIDE), BF)] * CTX,
        compiler_params=params(),
        cost_estimate=cost(100),
        name="attend_backward",
    )(saved, *grads)


def norm_body(
    group, attn_0, attn_1, attn_2, attn_3, resid, scale, shift, router, ids, place,
    send, kept, gate, inverse, hidden, stage,
):
    square = jnp.zeros((TOK, 1), F32)
    for s, attn in enumerate((attn_0, attn_1, attn_2, attn_3)):
        cols = group_cols(group, s)
        part = resid[:, cols].astype(F32) + attn[...].astype(F32)
        hidden[:, cols] = part
        square = square + jnp.sum(part * part, axis=1, keepdims=True)
    inv = lax.rsqrt(square / D + NORM_EPSILON)
    normed_mod = (hidden[...] * inv * (1.0 + scale[...]) + shift[...]).astype(BF)
    kept[...] = normed_mod
    inverse[...] = jnp.broadcast_to(inv, (TOK, 128))
    pick = (one_hot(place[:, 0:1], SLOTS) + one_hot(place[:, 1:2], SLOTS)).astype(BF)
    to_blocks(dot_rows(pick, normed_mod), stage, PLAIN)
    send[...] = stage[...].reshape(EXPERTS, PLAIN, 128).astype(BF)
    logits = dot_cols(normed_mod, router[...])
    hot = one_hot(ids[:, 0:1], EXPERTS) - one_hot(ids[:, 1:2], EXPERTS)
    margin = jnp.sum(logits * hot, axis=1, keepdims=True)
    gate[...] = jnp.broadcast_to(jax.nn.sigmoid(margin), (TOK, 128))


def send_rows(group, attn, resid, scale, shift, router, ids, place):
    return staged(
        norm_body,
        [group],
        [*attn, resid, scale, shift, router, ids, place],
        [
            hbm((EXPERTS, PLAIN, 128), BF),
            hbm((TOK, D), BF),
            hbm((TOK, 128), F32),
            hbm((TOK, 128), F32),
        ],
        "norm_dispatch",
        3,
        scratch=[pltpu.VMEM((TOK, D), F32), pltpu.VMEM((EXPERTS * PLAIN, 128), F32)],
    )


def gelu_terms(pre):
    square = pre * pre
    turn = jnp.tanh(GELU_C * (pre + 0.044715 * pre * square))
    return square, turn


def forward_body(
    arrived, arrived_grads, w_in, w_out, router, own,
    rows, row_grads, pre_out, y_send,
    stage, y_sum, branch_grad,
):
    step = pl.program_id(0)

    @pl.when(step == 0)
    def _():
        from_blocks(arrived_grads[:, 0:PLAIN, :], stage, branch_grad, PLAIN)
        from_blocks(arrived[...], stage, rows, PLAIN)
        partner_table = arrived_grads[:, PLAIN : PLAIN + 16, :].astype(F32)[:, 0, :]
        partner = jnp.concatenate(
            [partner_table[:, s : s + 1] for s in range(CAP)], axis=0
        ).astype(jnp.int32)
        logits = dot_cols(rows[...], router[...])
        margin = jnp.sum(logits * (own[...] - one_hot(partner, EXPERTS)), axis=1, keepdims=True)
        row_grads[...] = (jax.nn.sigmoid(margin) * branch_grad[...].astype(F32)).astype(BF)
        y_sum[...] = jnp.zeros_like(y_sum)

    pre = dot(rows[...], w_in[0])
    pre_out[0] = pre
    _, turn = gelu_terms(pre)
    act = (0.5 * pre * (1.0 + turn)).astype(BF)
    y_sum[...] += dot(act, w_out[0]).astype(BF).astype(F32)

    @pl.when(step == CTX - 1)
    def _():
        ref_to_blocks(y_sum, stage)
        y_send[...] = stage[...].reshape(EXPERTS, PLAIN, 128).astype(BF)


def whole(*dims):
    return pl.BlockSpec(dims, lambda b: (0,) * len(dims))


def of_block(*dims):
    return pl.BlockSpec((1,) + dims, lambda b: (b,) + (0,) * len(dims))


def experts_forward(arrived, arrived_grads, w_in, w_out, router, own):
    return pl.pallas_call(
        forward_body,
        grid=(CTX,),
        in_specs=[
            whole(EXPERTS, PLAIN, 128),
            whole(EXPERTS, TAGGED, 128),
            of_block(D, FF_BLOCK),
            of_block(FF_BLOCK, D),
            whole(EXPERTS, D),
            whole(1, EXPERTS),
        ],
        out_specs=[
            whole(SLOTS, D),
            whole(SLOTS, D),
            of_block(SLOTS, FF_BLOCK),
            whole(EXPERTS, PLAIN, 128),
        ],
        out_shape=[
            hbm((SLOTS, D), BF),
            hbm((SLOTS, D), BF),
            hbm((CTX, SLOTS, FF_BLOCK), F32),
            hbm((EXPERTS, PLAIN, 128), BF),
        ],
        scratch_shapes=[
            pltpu.VMEM((EXPERTS * PLAIN, 128), F32),
            pltpu.VMEM((SLOTS, D), F32),
            pltpu.VMEM((SLOTS, D), BF),
        ],
        compiler_params=params(60),
        cost_estimate=cost(10),
        name="expert_forward",
    )(arrived, arrived_grads, w_in, w_out, router, own)


def backward_body(rows, row_grads, pre_in, w_in, w_out, in_send, out_send, part_send, stage, part_sum):
    step = pl.program_id(0)

    @pl.when(step == 0)
    def _():
        part_sum[...] = jnp.zeros_like(part_sum)

    pre = pre_in[0]
    square, turn = gelu_terms(pre)
    act = (0.5 * pre * (1.0 + turn)).astype(BF)
    slope = 0.5 * (1.0 + turn) + 0.5 * pre * (1.0 - turn * turn) * (
        GELU_C * (1.0 + 3.0 * 0.044715 * square)
    )
    pre_grad = (dot_cols(row_grads[...], w_out[0]) * slope).astype(BF)
    part_sum[...] += dot_cols(pre_grad, w_in[0]).astype(BF).astype(F32)
    in_send[0] = dot_rows(rows[...], pre_grad).astype(BF)
    out_send[0] = dot_rows(act, row_grads[...]).astype(BF)

    @pl.when(step == CTX - 1)
    def _():
        ref_to_blocks(part_sum, stage)
        part_send[...] = stage[...].reshape(EXPERTS, PLAIN, 128).astype(BF)


def experts_backward(rows, row_grads, pre, w_in, w_out):
    return pl.pallas_call(
        backward_body,
        grid=(CTX,),
        in_specs=[
            whole(SLOTS, D),
            whole(SLOTS, D),
            of_block(SLOTS, FF_BLOCK),
            of_block(D, FF_BLOCK),
            of_block(FF_BLOCK, D),
        ],
        out_specs=[of_block(D, FF_BLOCK), of_block(FF_BLOCK, D), whole(EXPERTS, PLAIN, 128)],
        out_shape=[
            hbm((CTX, D, FF_BLOCK), BF),
            hbm((CTX, FF_BLOCK, D), BF),
            hbm((EXPERTS, PLAIN, 128), BF),
        ],
        scratch_shapes=[pltpu.VMEM((EXPERTS * PLAIN, 128), F32), pltpu.VMEM((SLOTS, D), F32)],
        compiler_params=params(60),
        cost_estimate=cost(15),
        name="expert_backward",
    )(rows, row_grads, pre, w_in, w_out)


def one_hots(ids):
    return one_hot(ids[:, 0:1], EXPERTS), one_hot(ids[:, 1:2], EXPERTS)


def resid_body(
    group, arrived, attn_0, attn_1, attn_2, attn_3, resid, grad_out, scale, router, place, logit_grad, inverse,
    resid_grad, send_0, send_1, send_2, send_3,
    stage, back, normed, lifted,
):
    from_blocks(arrived[...], stage, back, PLAIN)
    pick = (one_hot(place[:, 0:1], SLOTS) + one_hot(place[:, 1:2], SLOTS)).astype(BF)
    input_grad = dot(pick, back[...]) + dot(logit_grad[...], router[...])
    inv = inverse[:, 0:1]
    lifted[...] = input_grad * (1.0 + scale[...])
    mean = jnp.zeros((TOK, 1), F32)
    for s, attn in enumerate((attn_0, attn_1, attn_2, attn_3)):
        cols = group_cols(group, s)
        part = (resid[:, cols].astype(F32) + attn[...].astype(F32)) * inv
        normed[:, cols] = part
        mean = mean + jnp.sum(part * lifted[:, cols], axis=1, keepdims=True)
    mean = mean / D
    for s, send in enumerate((send_0, send_1, send_2, send_3)):
        cols = group_cols(group, s)
        part = grad_out[:, cols].astype(F32) + inv * (lifted[:, cols] - normed[:, cols] * mean)
        low_part = part.astype(BF)
        resid_grad[:, cols] = low_part
        send[...] = low_part


def resid_back(group, arrived, attn, resid, grad_out, scale, router, place, logit_grad, inverse, after):
    return staged(
        resid_body,
        [group],
        [arrived, *attn, resid, grad_out, scale, router, place, logit_grad, inverse],
        [hbm((TOK, D), BF)] + [hbm((TOK, WIDE), BF)] * CTX,
        "resid_backward",
        30,
        scratch=[
            pltpu.VMEM((EXPERTS * PLAIN, 128), F32),
            pltpu.VMEM((SLOTS, D), BF),
            pltpu.VMEM((TOK, D), F32),
            pltpu.VMEM((TOK, D), F32),
        ],
        unread=[after],
        mib=60,
    )


def mixed_body(
    group, own, arrived, attn_0, attn_1, attn_2, attn_3, resid, grad_out, mod_gate, ids, place, gate, kept,
    out, logit_out, router_0, router_1, router_2, router_3,
    stage, back, branch, twice,
):
    from_blocks(arrived[...], stage, back, PLAIN)
    gate_one = gate[:, 0:1]
    branch_grad = mod_gate[...] * grad_out[...].astype(F32)
    result_one = dot(one_hot(place[:, 0:1], SLOTS).astype(BF), back[...])
    pull = jnp.sum(branch_grad * result_one, axis=1, keepdims=True)
    result_two = dot(one_hot(place[:, 1:2], SLOTS).astype(BF), back[...])
    pull = pull - jnp.sum(branch_grad * result_two, axis=1, keepdims=True)
    first_hot, second_hot = one_hots(ids)
    tilt = pull * gate_one * (1.0 - gate_one)
    logit_grad = (tilt * (first_hot - second_hot)).astype(BF)
    logit_out[...] = logit_grad
    terms = dot_rows(logit_grad, kept[...])
    for c in range(CHUNKS):
        chunk = terms[:, c * 128 : (c + 1) * 128]
        twice[pl.ds(c, EXPERTS, stride=CHUNKS), :] = chunk
        twice[pl.ds(EXPERTS * CHUNKS + c, EXPERTS, stride=CHUNKS), :] = chunk
    for k, send in enumerate((router_0, router_1, router_2, router_3)):
        first = pl.multiple_of(own[0] * CHUNKS, CHUNKS) + k * ROUTER_QUARTER
        send[...] = twice[pl.ds(first, ROUTER_QUARTER), :]
    branch[...] = mod_gate[...] * (gate_one * result_one + (1.0 - gate_one) * result_two)
    for s, attn in enumerate((attn_0, attn_1, attn_2, attn_3)):
        cols = group_cols(group, s)
        hidden = resid[:, cols].astype(F32) + attn[...].astype(F32)
        out[:, cols] = (hidden + branch[:, cols]).astype(BF)


def mix(group, own, arrived, attn, resid, grad_out, mod_gate, ids, place, gate, kept):
    return staged(
        mixed_body,
        [group, own],
        [arrived, *attn, resid, grad_out, mod_gate, ids, place, gate, kept],
        [hbm((TOK, D), BF), hbm((TOK, EXPERTS), BF)] + [hbm((ROUTER_QUARTER, 128), F32)] * 4,
        "mixed_output",
        5,
        scratch=[
            pltpu.VMEM((EXPERTS * PLAIN, 128), F32),
            pltpu.VMEM((SLOTS, D), BF),
            pltpu.VMEM((TOK, D), F32),
            pltpu.VMEM((2 * EXPERTS * CHUNKS, 128), F32),
        ],
        mib=60,
    )


def router_body(own, part_0, part_1, part_2, part_3, out, twice):
    quarter = EXPERTS * CHUNKS // 4
    for i, part in enumerate((part_0, part_1, part_2, part_3)):
        twice[i * quarter : (i + 1) * quarter] = part[...]
        twice[(i + 4) * quarter : (i + 5) * quarter] = part[...]
    first = (EXPERTS - own[0]) * CHUNKS
    for c in range(CHUNKS):
        out[:, c * 128 : (c + 1) * 128] = twice[pl.ds(first + c, EXPERTS, stride=CHUNKS), :]


def add_four_body(*refs):
    total = refs[0][...] + refs[1][...] + refs[2][...] + refs[3][...]
    outs = refs[4:]
    rows = total.shape[0] // len(outs)
    for i, out in enumerate(outs):
        out[...] = total[i * rows : (i + 1) * rows]


def add_four(parts, pieces, after=()):
    rows = parts[0].shape[0] // pieces
    outs = [hbm((rows, 128), F32)] * pieces
    return staged(add_four_body, [], parts, outs, "add_four", 1, unread=after)


def order_router(own, parts):
    return staged(
        router_body,
        [own],
        parts,
        hbm((EXPERTS, D), F32),
        "order_router",
        2,
        scratch=[pltpu.VMEM((2 * EXPERTS * CHUNKS, 128), F32)],
    )


def swap(x):
    return lax.all_to_all(x, "expert", split_axis=0, concat_axis=0, tiled=True)


def shift(x, axis, count, step):
    return lax.ppermute(x, axis, [(i, (i + step) % count) for i in range(count)])


def around(parts, sign):
    return [parts[0]] + [shift(parts[s], "ctx", CTX, sign * s) for s in range(1, CTX)]


def spread(parts, digit):
    return [parts[0]] + [shift(parts[k], "expert", EXPERTS, k * digit) for k in range(1, 4)]


def local(
    resid, queries, keys, values, mod_scale, mod_shift, mod_gate, router, w_in, w_out, expert_ids, grad_out
):
    group = lax.axis_index("ctx").astype(jnp.int32)[None]
    expert = lax.axis_index("expert").astype(jnp.int32)
    own = (jnp.arange(EXPERTS, dtype=jnp.int32) == expert).astype(F32)[None, :]
    router_rows = router.T
    packed = pack(group, queries, keys, values)
    heads = around(packed, 1)
    place, grads = send_grads(grad_out, mod_gate, expert_ids, packed[0])
    arrived_grads = swap(grads)
    full_in = lax.all_gather(w_in, "ctx", axis=0, tiled=True)
    full_out = lax.all_gather(w_out, "ctx", axis=0, tiled=True)
    *attn_heads, saved = attend(heads)
    attn = around(attn_heads, -1)
    rows, kept, gate, inverse = send_rows(
        group, attn, resid, mod_scale, mod_shift, router_rows, expert_ids, place
    )
    arrived = swap(rows)
    flat_rows, flat_grads, pre_act, y_rows = experts_forward(
        arrived, arrived_grads, full_in, full_out, router_rows, own
    )
    outputs = swap(y_rows)
    in_terms, out_terms, part_rows = experts_backward(flat_rows, flat_grads, pre_act, full_in, full_out)
    parts = swap(part_rows)
    mixed_out, logit_grad, *router_terms = mix(
        group, expert[None], outputs, attn, resid, grad_out, mod_gate, expert_ids, place, gate, kept
    )
    in_terms, out_terms, _ = lax.optimization_barrier((in_terms, out_terms, outputs))
    grad_w_in, grad_w_out = (
        lax.psum_scatter(x, "ctx", scatter_dimension=0, tiled=True) for x in (in_terms, out_terms)
    )
    router_terms = add_four(spread(router_terms, 16), 4)
    resid_grad, *head_grads = resid_back(
        group, parts, attn, resid, grad_out, mod_scale, router_rows, place, logit_grad, inverse,
        router_terms[0],
    )
    attn_grads = around(head_grads, 1)
    head_terms = attend_back(saved, attn_grads)
    head_sums = around(head_terms, -1)
    *router_terms, _ = lax.optimization_barrier((*router_terms, *attn_grads[1:]))[:5]
    router_terms = add_four(spread(router_terms, 4), 4)
    router_terms = add_four(spread(router_terms, 1), 1)
    pieces = add_four(around(router_terms * CTX, 1), 1)[0]
    for digit in (1, 4, 16):
        quarters = spread([pieces] * 4, -digit)
        pieces = jnp.concatenate(quarters, axis=0)
    grad_router = order_router(expert[None], quarters).T
    grad_queries, grad_keys, grad_values = unpack(group, head_sums)
    return (
        mixed_out,
        resid_grad,
        grad_queries,
        grad_keys,
        grad_values,
        grad_w_in,
        grad_w_out,
        grad_router,
    )


def solution(mesh):
    tokens = P(("expert", "ctx"), None)
    clip = P("expert", None)
    return jax.shard_map(
        local,
        mesh=mesh,
        in_specs=(
            tokens, tokens, tokens, tokens, clip, clip, clip, P(),
            P("expert", None, "ctx"), P("expert", "ctx", None), tokens, tokens,
        ),
        out_specs=(
            tokens, tokens, tokens, tokens, tokens,
            P("expert", None, "ctx"), P("expert", "ctx", None), P(),
        ),
        check_vma=False,
    )
```

```python
import math

import jax
import jax.numpy as jnp
from jax import lax
from jax.experimental import pallas as pl
from jax.experimental.pallas import tpu as pltpu
from jax.sharding import PartitionSpec as P

D = 2048
HEADS = 16
HDIM = 128
EXPERTS = 64
TOK = 128
CTX = 4
CAP = 5
SLOTS = EXPERTS * CAP
CHUNKS = D // 128
WIDE = 512
FF_BLOCK = 256
PLAIN = CAP * CHUNKS
TAGGED = PLAIN + 16
NORM_EPSILON = 1e-06
SCORE_SCALE = 1.0 / math.sqrt(HDIM)
GELU_C = math.sqrt(2.0 / math.pi)
BF = jnp.bfloat16
F32 = jnp.float32


def params(mib=44):
    return pltpu.CompilerParams(vmem_limit_bytes=mib << 20)


def dot(a, b):
    return jnp.dot(a, b, preferred_element_type=F32)


def dot_rows(a, b):
    return lax.dot_general(a, b, (((0,), (0,)), ((), ())), preferred_element_type=F32)


def dot_cols(a, b):
    return lax.dot_general(a, b, (((1,), (1,)), ((), ())), preferred_element_type=F32)


def shape(dims, kind):
    return jax.ShapeDtypeStruct(dims, kind)


def hbm(dims, kind):
    return pltpu.HBM(dims, kind)


def cost(micros):
    return pl.CostEstimate(flops=0, transcendentals=0, bytes_accessed=int(micros * 3e6))


SCALAR = pl.BlockSpec(memory_space=pltpu.SMEM)
IN_HBM = pl.BlockSpec(memory_space=pltpu.HBM)
FULL = pl.BlockSpec(memory_space=pltpu.VMEM)


def staged(body, scalars, args, out_shape, name, micros, scratch=(), unread=(), mib=44, carried=None):
    outs = list(out_shape) if isinstance(out_shape, (list, tuple)) else [out_shape]
    extra = {}
    if carried is not None:
        unread = [*unread, carried]
        outs = outs + [hbm(carried.shape, carried.dtype)]
        out_shape = outs
        extra = {
            "out_specs": [FULL] * (len(outs) - 1) + [IN_HBM],
            "input_output_aliases": {len(scalars) + len(args) + len(unread) - 1: len(outs) - 1},
        }
    front, read = len(scalars) + len(args), len(scalars) + len(args) + len(unread)

    def kernel(*refs):
        results = refs[read : read + len(outs)]
        own = refs[read + len(outs) : read + len(outs) + len(scratch)]
        buffers = refs[read + len(outs) + len(scratch) : -1]
        copies = [
            pltpu.make_async_copy(source, buffer, refs[-1].at[i])
            for i, (source, buffer) in enumerate(zip(refs[len(scalars) : front], buffers))
        ]
        for copy in copies:
            copy.start()
        for copy in copies:
            copy.wait()
        body(*refs[: len(scalars)], *buffers, *results, *own)

    return pl.pallas_call(
        kernel,
        in_specs=[SCALAR] * len(scalars) + [IN_HBM] * (len(args) + len(unread)),
        out_shape=out_shape,
        scratch_shapes=list(scratch)
        + [pltpu.VMEM(x.shape, x.dtype) for x in args]
        + [pltpu.SemaphoreType.DMA((len(args),))],
        compiler_params=params(mib),
        cost_estimate=cost(micros),
        name=name,
        **extra,
    )(*scalars, *args, *unread)


def ref_to_blocks(rows, stage):
    @pl.loop(0, CAP)
    def _(s):
        for c in range(CHUNKS):
            stage[pl.ds(s * CHUNKS + c, EXPERTS, stride=PLAIN), :] = rows[
                pl.ds(pl.multiple_of(s * EXPERTS, EXPERTS), EXPERTS), c * 128 : (c + 1) * 128
            ]


def store_blocks(stage, blocks):
    @pl.loop(0, EXPERTS // 8)
    def _(i):
        rows = stage[pl.ds(pl.multiple_of(i * 8 * PLAIN, 8 * PLAIN), 8 * PLAIN), :]
        blocks[pl.ds(pl.multiple_of(i * 8, 8), 8)] = rows.reshape(8, PLAIN, 128).astype(BF)


def from_blocks(blocks, stage, rows, block):
    @pl.loop(0, EXPERTS // 8)
    def _(i):
        stage[pl.ds(pl.multiple_of(i * 8 * block, 8 * block), 8 * block), :] = (
            blocks[pl.ds(pl.multiple_of(i * 8, 8), 8)].astype(F32).reshape(8 * block, 128)
        )

    @pl.loop(0, CAP)
    def _(s):
        for c in range(CHUNKS):
            rows[pl.ds(pl.multiple_of(s * EXPERTS, EXPERTS), EXPERTS), c * 128 : (c + 1) * 128] = stage[
                pl.ds(s * CHUNKS + c, EXPERTS, stride=block), :
            ].astype(BF)


def one_hot(column, width):
    return (column == lax.broadcasted_iota(jnp.int32, (column.shape[0], width), 1)).astype(F32)


def group_cols(place, s):
    return pl.ds(pl.multiple_of(lax.rem(place[0] + s, CTX) * WIDE, WIDE), WIDE)


def pack_body(place, q, k, v, *outs):
    for s, out in enumerate(outs):
        cols = group_cols(place, s)
        out[0:TOK] = q[:, cols]
        out[TOK : 2 * TOK] = k[:, cols]
        out[2 * TOK :] = v[:, cols]


def pack(group, q, k, v):
    return staged(pack_body, [group], [q, k, v], [hbm((3 * TOK, WIDE), BF)] * CTX, "pack_heads", 3)


def unpack_body(place, *refs):
    dq, dk, dv = refs[CTX:]
    for s in range(CTX):
        x, cols = refs[s], group_cols(place, s)
        dq[:, cols] = x[0:TOK]
        dk[:, cols] = x[TOK : 2 * TOK]
        dv[:, cols] = x[2 * TOK :]


def unpack(group, parts):
    return staged(unpack_body, [group], parts, [hbm((TOK, D), BF)] * 3, "unpack_heads", 60)


def tagged_store(out, stage, tag_rows):
    store_blocks(stage, out.at[:, 0:PLAIN, :])
    row = lax.broadcasted_iota(jnp.int32, (EXPERTS, 16, 128), 1)
    tags = jnp.zeros((EXPERTS, 16, 128), F32)
    for i, tag in enumerate(tag_rows):
        tags = jnp.where(row == i, tag[:, None, :], tags)
    out[:, PLAIN:, :] = tags.astype(BF)


def slots_to_lanes(columns):
    lane = lax.broadcasted_iota(jnp.int32, (EXPERTS, 128), 1)
    table = jnp.zeros((EXPERTS, 128), F32)
    for s in range(CAP):
        table = jnp.where(lane == s, columns[s * EXPERTS : (s + 1) * EXPERTS], table)
    return table


def grads_body(grad_out, mod_gate, ids, place_out, send, stage, picked):
    first, second = ids[:, 0:1], ids[:, 1:2]
    first_hot, second_hot = one_hot(first, EXPERTS), one_hot(second, EXPERTS)
    both = first_hot + second_hot
    rows = lax.broadcasted_iota(jnp.int32, (TOK, TOK), 0)
    cols = lax.broadcasted_iota(jnp.int32, (TOK, TOK), 1)
    earlier = dot((cols < rows).astype(BF), both.astype(BF))
    pos_one = jnp.sum(earlier * first_hot, axis=1, keepdims=True).astype(jnp.int32)
    pos_two = jnp.sum(earlier * second_hot, axis=1, keepdims=True).astype(jnp.int32)
    place_one = pos_one * EXPERTS + first
    place_two = pos_two * EXPERTS + second
    lane = lax.broadcasted_iota(jnp.int32, (TOK, 2), 1)
    place_out[...] = jnp.where(lane == 0, place_one, place_two)
    pick_one = one_hot(place_one, SLOTS).astype(BF)
    pick_two = one_hot(place_two, SLOTS).astype(BF)
    branch_grad = (mod_gate[...] * grad_out[...].astype(F32)).astype(BF)
    picked[...] = dot_rows(pick_one + pick_two, branch_grad)
    ref_to_blocks(picked, stage)
    other_one = jnp.broadcast_to(second.astype(F32), (TOK, 128)).astype(BF)
    other_two = jnp.broadcast_to(first.astype(F32), (TOK, 128)).astype(BF)
    partner = dot_rows(pick_one, other_one) + dot_rows(pick_two, other_two)
    tagged_store(send, stage, [slots_to_lanes(partner)])


def send_grads(grad_out, mod_gate, ids, after):
    return staged(
        grads_body,
        [],
        [grad_out, mod_gate, ids],
        [hbm((TOK, 2), jnp.int32), hbm((EXPERTS, TAGGED, 128), BF)],
        "dispatch_grads",
        3,
        scratch=[pltpu.VMEM((EXPERTS * PLAIN, 128), F32), pltpu.VMEM((SLOTS, D), F32)],
        unread=[after],
    )


def heads_of(parts, which):
    return jnp.concatenate([x[which * TOK : (which + 1) * TOK, :] for x in parts], axis=0)


def attend_body(*refs):
    parts, outs, saved = refs[:CTX], refs[CTX : 2 * CTX], refs[2 * CTX]
    q, k, v = heads_of(parts, 0), heads_of(parts, 1), heads_of(parts, 2)
    scores = dot_cols(q, k) * SCORE_SCALE
    top = jnp.max(scores, axis=1, keepdims=True)
    weights = jnp.exp(scores - top)
    total = jnp.sum(weights, axis=1, keepdims=True)
    mixed = (dot(weights.astype(BF), v) / total).astype(BF)
    for i, x in enumerate((q, k, v, mixed)):
        saved[i] = x
    for s, out in enumerate(outs):
        out[...] = mixed[s * TOK : (s + 1) * TOK]


ONE_HEAD = pl.BlockSpec((TOK, HDIM), lambda h: (0, h))
THREE_HEADS = pl.BlockSpec((3 * TOK, HDIM), lambda h: (0, h))
SAVED = pl.BlockSpec((4, CTX * TOK, HDIM), lambda h: (0, 0, h))


def attend(parts):
    return pl.pallas_call(
        attend_body,
        grid=(WIDE // HDIM,),
        in_specs=[THREE_HEADS] * CTX,
        out_specs=[ONE_HEAD] * CTX + [SAVED],
        out_shape=[hbm((TOK, WIDE), BF)] * CTX + [hbm((4, CTX * TOK, WIDE), BF)],
        compiler_params=params(),
        cost_estimate=cost(10),
        name="attend_forward",
    )(*parts)


def attend_back_body(saved, *refs):
    grads, outs = refs[:CTX], refs[CTX:]
    q, k, v, o = (saved[i] for i in range(4))
    g = heads_of(grads, 0)
    scores = dot_cols(q, k) * SCORE_SCALE
    top = jnp.max(scores, axis=1, keepdims=True)
    total = jnp.sum(jnp.exp(scores - top), axis=1, keepdims=True)
    prob = jnp.exp(scores - (top + jnp.log(total)))
    row_dot = jnp.sum(g.astype(F32) * o.astype(F32), axis=1, keepdims=True)
    score_grad = (prob * (dot_cols(g, v) - row_dot)).astype(BF)
    dq = (dot(score_grad, k) * SCORE_SCALE).astype(BF)
    dk = (dot_rows(score_grad, q) * SCORE_SCALE).astype(BF)
    dv = dot_rows(prob.astype(BF), g).astype(BF)
    for s, out in enumerate(outs):
        rows = slice(s * TOK, (s + 1) * TOK)
        out[0:TOK] = dq[rows]
        out[TOK : 2 * TOK] = dk[rows]
        out[2 * TOK :] = dv[rows]


def attend_back(saved, grads):
    return pl.pallas_call(
        attend_back_body,
        grid=(WIDE // HDIM,),
        in_specs=[SAVED] + [ONE_HEAD] * CTX,
        out_specs=[THREE_HEADS] * CTX,
        out_shape=[hbm((3 * TOK, WIDE), BF)] * CTX,
        compiler_params=params(),
        cost_estimate=cost(100),
        name="attend_backward",
    )(saved, *grads)


def norm_body(
    group, attn_0, attn_1, attn_2, attn_3, resid, scale, shift, router, ids, place,
    send, kept, gate, inverse, hidden, stage, picked,
):
    square = jnp.zeros((TOK, 1), F32)
    for s, attn in enumerate((attn_0, attn_1, attn_2, attn_3)):
        cols = group_cols(group, s)
        part = resid[:, cols].astype(F32) + attn[...].astype(F32)
        hidden[:, cols] = part
        square = square + jnp.sum(part * part, axis=1, keepdims=True)
    inv = lax.rsqrt(square / D + NORM_EPSILON)
    normed_mod = (hidden[...] * inv * (1.0 + scale[...]) + shift[...]).astype(BF)
    kept[...] = normed_mod
    inverse[...] = jnp.broadcast_to(inv, (TOK, 128))
    pick = (one_hot(place[:, 0:1], SLOTS) + one_hot(place[:, 1:2], SLOTS)).astype(BF)
    picked[...] = dot_rows(pick, normed_mod)
    ref_to_blocks(picked, stage)
    store_blocks(stage, send)
    logits = dot_cols(normed_mod, router[...])
    hot = one_hot(ids[:, 0:1], EXPERTS) - one_hot(ids[:, 1:2], EXPERTS)
    margin = jnp.sum(logits * hot, axis=1, keepdims=True)
    gate[...] = jnp.broadcast_to(jax.nn.sigmoid(margin), (TOK, 128))


def send_rows(group, attn, resid, scale, shift, router, ids, place):
    return staged(
        norm_body,
        [group],
        [*attn, resid, scale, shift, router, ids, place],
        [
            hbm((EXPERTS, PLAIN, 128), BF),
            hbm((TOK, D), BF),
            hbm((TOK, 128), F32),
            hbm((TOK, 128), F32),
        ],
        "norm_dispatch",
        3,
        scratch=[
            pltpu.VMEM((TOK, D), F32),
            pltpu.VMEM((EXPERTS * PLAIN, 128), F32),
            pltpu.VMEM((SLOTS, D), F32),
        ],
    )


def gelu_terms(pre):
    square = pre * pre
    turn = jnp.tanh(GELU_C * (pre + 0.044715 * pre * square))
    return square, turn


def forward_body(
    arrived, arrived_grads, w_in, w_out, router, own,
    rows, row_grads, pre_out, y_send,
    stage, y_sum, branch_grad,
):
    step = pl.program_id(0)

    @pl.when(step == 0)
    def _():
        from_blocks(arrived_grads.at[:, 0:PLAIN, :], stage, branch_grad, PLAIN)
        from_blocks(arrived, stage, rows, PLAIN)
        partner_table = arrived_grads[:, PLAIN : PLAIN + 16, :].astype(F32)[:, 0, :]
        partner = jnp.concatenate(
            [partner_table[:, s : s + 1] for s in range(CAP)], axis=0
        ).astype(jnp.int32)
        logits = dot_cols(rows[...], router[...])
        margin = jnp.sum(logits * (own[...] - one_hot(partner, EXPERTS)), axis=1, keepdims=True)
        row_grads[...] = (jax.nn.sigmoid(margin) * branch_grad[...].astype(F32)).astype(BF)
        y_sum[...] = jnp.zeros_like(y_sum)

    pre = dot(rows[...], w_in[0])
    pre_out[0] = pre
    _, turn = gelu_terms(pre)
    act = (0.5 * pre * (1.0 + turn)).astype(BF)
    y_sum[...] += dot(act, w_out[0]).astype(BF).astype(F32)

    @pl.when(step == CTX - 1)
    def _():
        ref_to_blocks(y_sum, stage)
        store_blocks(stage, y_send)


def whole(*dims):
    return pl.BlockSpec(dims, lambda b: (0,) * len(dims))


def of_block(*dims):
    return pl.BlockSpec((1,) + dims, lambda b: (b,) + (0,) * len(dims))


def experts_forward(arrived, arrived_grads, w_in, w_out, router, own):
    return pl.pallas_call(
        forward_body,
        grid=(CTX,),
        in_specs=[
            whole(EXPERTS, PLAIN, 128),
            whole(EXPERTS, TAGGED, 128),
            of_block(D, FF_BLOCK),
            of_block(FF_BLOCK, D),
            whole(EXPERTS, D),
            whole(1, EXPERTS),
        ],
        out_specs=[
            whole(SLOTS, D),
            whole(SLOTS, D),
            of_block(SLOTS, FF_BLOCK),
            whole(EXPERTS, PLAIN, 128),
        ],
        out_shape=[
            hbm((SLOTS, D), BF),
            hbm((SLOTS, D), BF),
            hbm((CTX, SLOTS, FF_BLOCK), F32),
            hbm((EXPERTS, PLAIN, 128), BF),
        ],
        scratch_shapes=[
            pltpu.VMEM((EXPERTS * PLAIN, 128), F32),
            pltpu.VMEM((SLOTS, D), F32),
            pltpu.VMEM((SLOTS, D), BF),
        ],
        compiler_params=params(60),
        cost_estimate=cost(10),
        name="expert_forward",
    )(arrived, arrived_grads, w_in, w_out, router, own)


def backward_body(rows, row_grads, pre_in, w_in, w_out, in_send, out_send, part_send, stage, part_sum):
    step = pl.program_id(0)

    @pl.when(step == 0)
    def _():
        part_sum[...] = jnp.zeros_like(part_sum)

    pre = pre_in[0]
    square, turn = gelu_terms(pre)
    act = (0.5 * pre * (1.0 + turn)).astype(BF)
    slope = 0.5 * (1.0 + turn) + 0.5 * pre * (1.0 - turn * turn) * (
        GELU_C * (1.0 + 3.0 * 0.044715 * square)
    )
    pre_grad = (dot_cols(row_grads[...], w_out[0]) * slope).astype(BF)
    part_sum[...] += dot_cols(pre_grad, w_in[0]).astype(BF).astype(F32)
    in_send[0] = dot_rows(rows[...], pre_grad).astype(BF)
    out_send[0] = dot_rows(act, row_grads[...]).astype(BF)

    @pl.when(step == CTX - 1)
    def _():
        ref_to_blocks(part_sum, stage)
        store_blocks(stage, part_send.at[:, 0:PLAIN, :])
        part_send[:, PLAIN:, :] = jnp.zeros((EXPERTS, CHUNKS, 128), BF)


def experts_backward(rows, row_grads, pre, w_in, w_out):
    return pl.pallas_call(
        backward_body,
        grid=(CTX,),
        in_specs=[
            whole(SLOTS, D),
            whole(SLOTS, D),
            of_block(SLOTS, FF_BLOCK),
            of_block(D, FF_BLOCK),
            of_block(FF_BLOCK, D),
        ],
        out_specs=[of_block(D, FF_BLOCK), of_block(FF_BLOCK, D), whole(EXPERTS, TAGGED, 128)],
        out_shape=[
            hbm((CTX, D, FF_BLOCK), BF),
            hbm((CTX, FF_BLOCK, D), BF),
            hbm((EXPERTS, TAGGED, 128), BF),
        ],
        scratch_shapes=[pltpu.VMEM((EXPERTS * PLAIN, 128), F32), pltpu.VMEM((SLOTS, D), F32)],
        compiler_params=params(60),
        cost_estimate=cost(15),
        name="expert_backward",
    )(rows, row_grads, pre, w_in, w_out)


def one_hots(ids):
    return one_hot(ids[:, 0:1], EXPERTS), one_hot(ids[:, 1:2], EXPERTS)


def resid_body(
    group, arrived, attn_0, attn_1, attn_2, attn_3, resid, grad_out, scale, router, place, logit_grad, inverse,
    resid_grad, router_column, send_0, send_1, send_2, send_3,
    stage, back, normed, lifted,
):
    from_blocks(arrived.at[:, 0:PLAIN, :], stage, back, PLAIN)
    router_column[...] = jnp.sum(arrived[:, PLAIN:TAGGED, :].astype(F32), axis=0)
    pick = (one_hot(place[:, 0:1], SLOTS) + one_hot(place[:, 1:2], SLOTS)).astype(BF)
    input_grad = dot(pick, back[...]) + dot(logit_grad[...], router[...])
    inv = inverse[:, 0:1]
    lifted[...] = input_grad * (1.0 + scale[...])
    mean = jnp.zeros((TOK, 1), F32)
    for s, attn in enumerate((attn_0, attn_1, attn_2, attn_3)):
        cols = group_cols(group, s)
        part = (resid[:, cols].astype(F32) + attn[...].astype(F32)) * inv
        normed[:, cols] = part
        mean = mean + jnp.sum(part * lifted[:, cols], axis=1, keepdims=True)
    mean = mean / D
    for s, send in enumerate((send_0, send_1, send_2, send_3)):
        cols = group_cols(group, s)
        part = grad_out[:, cols].astype(F32) + inv * (lifted[:, cols] - normed[:, cols] * mean)
        low_part = part.astype(BF)
        resid_grad[:, cols] = low_part
        send[...] = low_part


def resid_back(group, arrived, attn, resid, grad_out, scale, router, place, logit_grad, inverse):
    return staged(
        resid_body,
        [group],
        [arrived, *attn, resid, grad_out, scale, router, place, logit_grad, inverse],
        [hbm((TOK, D), BF), hbm((CHUNKS, 128), F32)] + [hbm((TOK, WIDE), BF)] * CTX,
        "resid_backward",
        30,
        scratch=[
            pltpu.VMEM((EXPERTS * PLAIN, 128), F32),
            pltpu.VMEM((SLOTS, D), BF),
            pltpu.VMEM((TOK, D), F32),
            pltpu.VMEM((TOK, D), F32),
        ],
        mib=60,
    )


def mixed_body(
    group, arrived, attn_0, attn_1, attn_2, attn_3, resid, grad_out, mod_gate, ids, place, gate, kept,
    out, logit_out, part_send,
    stage, back, branch, terms_blocks, sent_terms, sent,
):
    from_blocks(arrived, stage, back, PLAIN)
    gate_one = gate[:, 0:1]
    branch_grad = mod_gate[...] * grad_out[...].astype(F32)
    result_one = dot(one_hot(place[:, 0:1], SLOTS).astype(BF), back[...])
    pull = jnp.sum(branch_grad * result_one, axis=1, keepdims=True)
    result_two = dot(one_hot(place[:, 1:2], SLOTS).astype(BF), back[...])
    pull = pull - jnp.sum(branch_grad * result_two, axis=1, keepdims=True)
    first_hot, second_hot = one_hots(ids)
    tilt = pull * gate_one * (1.0 - gate_one)
    logit_grad = (tilt * (first_hot - second_hot)).astype(BF)
    logit_out[...] = logit_grad
    terms = dot_rows(logit_grad, kept[...])
    for c in range(CHUNKS):
        terms_blocks[pl.ds(c, EXPERTS, stride=CHUNKS), :] = terms[:, c * 128 : (c + 1) * 128]
    sent_terms[...] = terms_blocks[...].reshape(EXPERTS, CHUNKS, 128).astype(BF)
    copy = pltpu.make_async_copy(sent_terms, part_send.at[:, PLAIN:TAGGED, :], sent.at[0])
    copy.start()
    branch[...] = mod_gate[...] * (gate_one * result_one + (1.0 - gate_one) * result_two)
    for s, attn in enumerate((attn_0, attn_1, attn_2, attn_3)):
        cols = group_cols(group, s)
        hidden = resid[:, cols].astype(F32) + attn[...].astype(F32)
        out[:, cols] = (hidden + branch[:, cols]).astype(BF)
    copy.wait()


def mix(group, arrived, attn, resid, grad_out, mod_gate, ids, place, gate, kept, part_rows):
    return staged(
        mixed_body,
        [group],
        [arrived, *attn, resid, grad_out, mod_gate, ids, place, gate, kept],
        [hbm((TOK, D), BF), hbm((TOK, EXPERTS), BF)],
        "mixed_output",
        5,
        scratch=[
            pltpu.VMEM((EXPERTS * PLAIN, 128), F32),
            pltpu.VMEM((SLOTS, D), BF),
            pltpu.VMEM((TOK, D), F32),
            pltpu.VMEM((EXPERTS * CHUNKS, 128), F32),
            pltpu.VMEM((EXPERTS, CHUNKS, 128), BF),
            pltpu.SemaphoreType.DMA((1,)),
        ],
        mib=60,
        carried=part_rows,
    )


def order_body(blocks, out, stage):
    stage[...] = blocks[...].reshape(EXPERTS * CHUNKS, 128)
    for c in range(CHUNKS):
        out[:, c * 128 : (c + 1) * 128] = stage[pl.ds(c, EXPERTS, stride=CHUNKS), :]


def order_router(blocks):
    return staged(
        order_body,
        [],
        [blocks],
        hbm((EXPERTS, D), F32),
        "order_router",
        2,
        scratch=[pltpu.VMEM((EXPERTS * CHUNKS, 128), F32)],
    )


def swap(x):
    return lax.all_to_all(x, "expert", split_axis=0, concat_axis=0, tiled=True)


def shift(x, axis, count, step):
    return lax.ppermute(x, axis, [(i, (i + step) % count) for i in range(count)])


def around(parts, sign):
    return [parts[0]] + [shift(parts[s], "ctx", CTX, sign * s) for s in range(1, CTX)]


def local(
    resid, queries, keys, values, mod_scale, mod_shift, mod_gate, router, w_in, w_out, expert_ids, grad_out
):
    group = lax.axis_index("ctx").astype(jnp.int32)[None]
    expert = lax.axis_index("expert").astype(jnp.int32)
    own = (jnp.arange(EXPERTS, dtype=jnp.int32) == expert).astype(F32)[None, :]
    router_rows = router.T
    packed = pack(group, queries, keys, values)
    heads = around(packed, 1)
    place, grads = send_grads(grad_out, mod_gate, expert_ids, packed[0])
    arrived_grads = swap(grads)
    full_in = lax.all_gather(w_in, "ctx", axis=0, tiled=True)
    full_out = lax.all_gather(w_out, "ctx", axis=0, tiled=True)
    *attn_heads, saved = attend(heads)
    attn = around(attn_heads, -1)
    rows, kept, gate, inverse = send_rows(
        group, attn, resid, mod_scale, mod_shift, router_rows, expert_ids, place
    )
    arrived = swap(rows)
    flat_rows, flat_grads, pre_act, y_rows = experts_forward(
        arrived, arrived_grads, full_in, full_out, router_rows, own
    )
    outputs = swap(y_rows)
    in_terms, out_terms, part_rows = experts_backward(flat_rows, flat_grads, pre_act, full_in, full_out)
    in_terms, out_terms, _ = lax.optimization_barrier((in_terms, out_terms, outputs))
    grad_w_in, grad_w_out = (
        lax.psum_scatter(x, "ctx", scatter_dimension=0, tiled=True) for x in (in_terms, out_terms)
    )
    mixed_out, logit_grad, part_rows = mix(
        group, outputs, attn, resid, grad_out, mod_gate, expert_ids, place, gate, kept, part_rows
    )
    parts = swap(part_rows)
    resid_grad, router_column, *head_grads = resid_back(
        group, parts, attn, resid, grad_out, mod_scale, router_rows, place, logit_grad, inverse
    )
    attn_grads = around(head_grads, 1)
    head_terms = attend_back(saved, attn_grads)
    head_sums = around(head_terms, -1)
    router_column, *_ = lax.optimization_barrier((router_column, *attn_grads[1:]))
    *columns, _ = lax.optimization_barrier((*around([router_column] * CTX, 1), head_terms[0]))
    router_column = columns[0] + columns[1] + columns[2] + columns[3]
    grad_router = order_router(
        swap(jnp.broadcast_to(router_column, (EXPERTS, CHUNKS, 128)))
    ).T
    grad_queries, grad_keys, grad_values = unpack(group, head_sums)
    return (
        mixed_out,
        resid_grad,
        grad_queries,
        grad_keys,
        grad_values,
        grad_w_in,
        grad_w_out,
        grad_router,
    )


def solution(mesh):
    tokens = P(("expert", "ctx"), None)
    clip = P("expert", None)
    return jax.shard_map(
        local,
        mesh=mesh,
        in_specs=(
            tokens, tokens, tokens, tokens, clip, clip, clip, P(),
            P("expert", None, "ctx"), P("expert", "ctx", None), tokens, tokens,
        ),
        out_specs=(
            tokens, tokens, tokens, tokens, tokens,
            P("expert", None, "ctx"), P("expert", "ctx", None), P(),
        ),
        check_vma=False,
    )
```

```python
import math

import jax
import jax.numpy as jnp
from jax import lax
from jax.experimental import pallas as pl
from jax.experimental.pallas import tpu as pltpu
from jax.sharding import PartitionSpec as P

D = 2048
HEADS = 16
HDIM = 128
EXPERTS = 64
TOK = 128
CTX = 4
CAP = 5
SLOTS = EXPERTS * CAP
CHUNKS = D // 128
WIDE = 512
FF_BLOCK = 256
PLAIN = CAP * CHUNKS
TAGGED = PLAIN + 16
NORM_EPSILON = 1e-06
SCORE_SCALE = 1.0 / math.sqrt(HDIM)
GELU_C = math.sqrt(2.0 / math.pi)
BF = jnp.bfloat16
F32 = jnp.float32


def params(mib=44):
    return pltpu.CompilerParams(vmem_limit_bytes=mib << 20)


def dot(a, b):
    return jnp.dot(a, b, preferred_element_type=F32)


def dot_rows(a, b):
    return lax.dot_general(a, b, (((0,), (0,)), ((), ())), preferred_element_type=F32)


def dot_cols(a, b):
    return lax.dot_general(a, b, (((1,), (1,)), ((), ())), preferred_element_type=F32)


def shape(dims, kind):
    return jax.ShapeDtypeStruct(dims, kind)


def hbm(dims, kind):
    return pltpu.HBM(dims, kind)


def cost(micros):
    return pl.CostEstimate(flops=0, transcendentals=0, bytes_accessed=int(micros * 3e6))


SCALAR = pl.BlockSpec(memory_space=pltpu.SMEM)
IN_HBM = pl.BlockSpec(memory_space=pltpu.HBM)
FULL = pl.BlockSpec(memory_space=pltpu.VMEM)


def staged(body, scalars, args, out_shape, name, micros, scratch=(), unread=(), mib=44, carried=None):
    outs = list(out_shape) if isinstance(out_shape, (list, tuple)) else [out_shape]
    extra = {}
    if carried is not None:
        unread = [*unread, carried]
        outs = outs + [hbm(carried.shape, carried.dtype)]
        out_shape = outs
        extra = {
            "out_specs": [FULL] * (len(outs) - 1) + [IN_HBM],
            "input_output_aliases": {len(scalars) + len(args) + len(unread) - 1: len(outs) - 1},
        }
    front, read = len(scalars) + len(args), len(scalars) + len(args) + len(unread)

    def kernel(*refs):
        results = refs[read : read + len(outs)]
        own = refs[read + len(outs) : read + len(outs) + len(scratch)]
        buffers = refs[read + len(outs) + len(scratch) : -1]
        copies = [
            pltpu.make_async_copy(source, buffer, refs[-1].at[i])
            for i, (source, buffer) in enumerate(zip(refs[len(scalars) : front], buffers))
        ]
        for copy in copies:
            copy.start()
        for copy in copies:
            copy.wait()
        body(*refs[: len(scalars)], *buffers, *results, *own)

    return pl.pallas_call(
        kernel,
        in_specs=[SCALAR] * len(scalars) + [IN_HBM] * (len(args) + len(unread)),
        out_shape=out_shape,
        scratch_shapes=list(scratch)
        + [pltpu.VMEM(x.shape, x.dtype) for x in args]
        + [pltpu.SemaphoreType.DMA((len(args),))],
        compiler_params=params(mib),
        cost_estimate=cost(micros),
        name=name,
        **extra,
    )(*scalars, *args, *unread)


def ref_to_blocks(rows, stage):
    @pl.loop(0, CAP)
    def _(s):
        for c in range(CHUNKS):
            stage[pl.ds(s * CHUNKS + c, EXPERTS, stride=PLAIN), :] = rows[
                pl.ds(pl.multiple_of(s * EXPERTS, EXPERTS), EXPERTS), c * 128 : (c + 1) * 128
            ]


def store_blocks(stage, blocks):
    @pl.loop(0, EXPERTS // 8)
    def _(i):
        rows = stage[pl.ds(pl.multiple_of(i * 8 * PLAIN, 8 * PLAIN), 8 * PLAIN), :]
        blocks[pl.ds(pl.multiple_of(i * 8, 8), 8)] = rows.reshape(8, PLAIN, 128).astype(BF)


def from_blocks(blocks, stage, rows, block):
    @pl.loop(0, EXPERTS // 8)
    def _(i):
        stage[pl.ds(pl.multiple_of(i * 8 * block, 8 * block), 8 * block), :] = (
            blocks[pl.ds(pl.multiple_of(i * 8, 8), 8)].astype(F32).reshape(8 * block, 128)
        )

    @pl.loop(0, CAP)
    def _(s):
        for c in range(CHUNKS):
            rows[pl.ds(pl.multiple_of(s * EXPERTS, EXPERTS), EXPERTS), c * 128 : (c + 1) * 128] = stage[
                pl.ds(s * CHUNKS + c, EXPERTS, stride=block), :
            ].astype(BF)


def one_hot(column, width):
    return (column == lax.broadcasted_iota(jnp.int32, (column.shape[0], width), 1)).astype(F32)


def group_cols(place, s):
    return pl.ds(pl.multiple_of(lax.rem(place[0] + s, CTX) * WIDE, WIDE), WIDE)


def pack_body(place, q, k, v, *outs):
    for s, out in enumerate(outs):
        cols = group_cols(place, s)
        out[0:TOK] = q[:, cols]
        out[TOK : 2 * TOK] = k[:, cols]
        out[2 * TOK :] = v[:, cols]


def pack(group, q, k, v):
    return staged(pack_body, [group], [q, k, v], [hbm((3 * TOK, WIDE), BF)] * CTX, "pack_heads", 3)


def unpack_body(place, *refs):
    dq, dk, dv = refs[CTX:]
    for s in range(CTX):
        x, cols = refs[s], group_cols(place, s)
        dq[:, cols] = x[0:TOK]
        dk[:, cols] = x[TOK : 2 * TOK]
        dv[:, cols] = x[2 * TOK :]


def unpack(group, parts):
    return staged(unpack_body, [group], parts, [hbm((TOK, D), BF)] * 3, "unpack_heads", 60)


def tagged_store(out, stage, tag_rows):
    store_blocks(stage, out.at[:, 0:PLAIN, :])
    row = lax.broadcasted_iota(jnp.int32, (EXPERTS, 16, 128), 1)
    tags = jnp.zeros((EXPERTS, 16, 128), F32)
    for i, tag in enumerate(tag_rows):
        tags = jnp.where(row == i, tag[:, None, :], tags)
    out[:, PLAIN:, :] = tags.astype(BF)


def slots_to_lanes(columns):
    lane = lax.broadcasted_iota(jnp.int32, (EXPERTS, 128), 1)
    table = jnp.zeros((EXPERTS, 128), F32)
    for s in range(CAP):
        table = jnp.where(lane == s, columns[s * EXPERTS : (s + 1) * EXPERTS], table)
    return table


def grads_body(grad_out, mod_gate, ids, place_out, send, stage, picked):
    first, second = ids[:, 0:1], ids[:, 1:2]
    first_hot, second_hot = one_hot(first, EXPERTS), one_hot(second, EXPERTS)
    both = first_hot + second_hot
    rows = lax.broadcasted_iota(jnp.int32, (TOK, TOK), 0)
    cols = lax.broadcasted_iota(jnp.int32, (TOK, TOK), 1)
    earlier = dot((cols < rows).astype(BF), both.astype(BF))
    pos_one = jnp.sum(earlier * first_hot, axis=1, keepdims=True).astype(jnp.int32)
    pos_two = jnp.sum(earlier * second_hot, axis=1, keepdims=True).astype(jnp.int32)
    place_one = pos_one * EXPERTS + first
    place_two = pos_two * EXPERTS + second
    lane = lax.broadcasted_iota(jnp.int32, (TOK, 2), 1)
    place_out[...] = jnp.where(lane == 0, place_one, place_two)
    pick_one = one_hot(place_one, SLOTS).astype(BF)
    pick_two = one_hot(place_two, SLOTS).astype(BF)
    branch_grad = (mod_gate[...] * grad_out[...].astype(F32)).astype(BF)
    picked[...] = dot_rows(pick_one + pick_two, branch_grad)
    ref_to_blocks(picked, stage)
    other_one = jnp.broadcast_to(second.astype(F32), (TOK, 128)).astype(BF)
    other_two = jnp.broadcast_to(first.astype(F32), (TOK, 128)).astype(BF)
    partner = dot_rows(pick_one, other_one) + dot_rows(pick_two, other_two)
    tagged_store(send, stage, [slots_to_lanes(partner)])


def send_grads(grad_out, mod_gate, ids, after):
    return staged(
        grads_body,
        [],
        [grad_out, mod_gate, ids],
        [hbm((TOK, 2), jnp.int32), hbm((EXPERTS, TAGGED, 128), BF)],
        "dispatch_grads",
        3,
        scratch=[pltpu.VMEM((EXPERTS * PLAIN, 128), F32), pltpu.VMEM((SLOTS, D), F32)],
        unread=[after],
    )


def heads_of(parts, which):
    return jnp.concatenate([x[which * TOK : (which + 1) * TOK, :] for x in parts], axis=0)


def attend_body(*refs):
    parts, outs, saved = refs[:CTX], refs[CTX : 2 * CTX], refs[2 * CTX]
    q, k, v = heads_of(parts, 0), heads_of(parts, 1), heads_of(parts, 2)
    scores = dot_cols(q, k) * SCORE_SCALE
    top = jnp.max(scores, axis=1, keepdims=True)
    weights = jnp.exp(scores - top)
    total = jnp.sum(weights, axis=1, keepdims=True)
    mixed = (dot(weights.astype(BF), v) / total).astype(BF)
    for i, x in enumerate((q, k, v, mixed)):
        saved[i] = x
    for s, out in enumerate(outs):
        out[...] = mixed[s * TOK : (s + 1) * TOK]


ONE_HEAD = pl.BlockSpec((TOK, HDIM), lambda h: (0, h))
THREE_HEADS = pl.BlockSpec((3 * TOK, HDIM), lambda h: (0, h))
SAVED = pl.BlockSpec((4, CTX * TOK, HDIM), lambda h: (0, 0, h))


def attend(parts):
    return pl.pallas_call(
        attend_body,
        grid=(WIDE // HDIM,),
        in_specs=[THREE_HEADS] * CTX,
        out_specs=[ONE_HEAD] * CTX + [SAVED],
        out_shape=[hbm((TOK, WIDE), BF)] * CTX + [hbm((4, CTX * TOK, WIDE), BF)],
        compiler_params=params(),
        cost_estimate=cost(10),
        name="attend_forward",
    )(*parts)


def attend_back_body(saved, *refs):
    grads, outs = refs[:CTX], refs[CTX:]
    q, k, v, o = (saved[i] for i in range(4))
    g = heads_of(grads, 0)
    scores = dot_cols(q, k) * SCORE_SCALE
    top = jnp.max(scores, axis=1, keepdims=True)
    total = jnp.sum(jnp.exp(scores - top), axis=1, keepdims=True)
    prob = jnp.exp(scores - (top + jnp.log(total)))
    row_dot = jnp.sum(g.astype(F32) * o.astype(F32), axis=1, keepdims=True)
    score_grad = (prob * (dot_cols(g, v) - row_dot)).astype(BF)
    dq = (dot(score_grad, k) * SCORE_SCALE).astype(BF)
    dk = (dot_rows(score_grad, q) * SCORE_SCALE).astype(BF)
    dv = dot_rows(prob.astype(BF), g).astype(BF)
    for s, out in enumerate(outs):
        rows = slice(s * TOK, (s + 1) * TOK)
        out[0:TOK] = dq[rows]
        out[TOK : 2 * TOK] = dk[rows]
        out[2 * TOK :] = dv[rows]


def attend_back(saved, grads):
    return pl.pallas_call(
        attend_back_body,
        grid=(WIDE // HDIM,),
        in_specs=[SAVED] + [ONE_HEAD] * CTX,
        out_specs=[THREE_HEADS] * CTX,
        out_shape=[hbm((3 * TOK, WIDE), BF)] * CTX,
        compiler_params=params(),
        cost_estimate=cost(100),
        name="attend_backward",
    )(saved, *grads)


def norm_body(
    group, attn_0, attn_1, attn_2, attn_3, resid, scale, shift, router, ids, place,
    send, kept, gate, inverse, hidden, stage, picked,
):
    square = jnp.zeros((TOK, 1), F32)
    for s, attn in enumerate((attn_0, attn_1, attn_2, attn_3)):
        cols = group_cols(group, s)
        part = resid[:, cols].astype(F32) + attn[...].astype(F32)
        hidden[:, cols] = part
        square = square + jnp.sum(part * part, axis=1, keepdims=True)
    inv = lax.rsqrt(square / D + NORM_EPSILON)
    normed_mod = (hidden[...] * inv * (1.0 + scale[...]) + shift[...]).astype(BF)
    kept[...] = normed_mod
    inverse[...] = jnp.broadcast_to(inv, (TOK, 128))
    pick = (one_hot(place[:, 0:1], SLOTS) + one_hot(place[:, 1:2], SLOTS)).astype(BF)
    picked[...] = dot_rows(pick, normed_mod)
    ref_to_blocks(picked, stage)
    store_blocks(stage, send)
    logits = dot_cols(normed_mod, router[...])
    hot = one_hot(ids[:, 0:1], EXPERTS) - one_hot(ids[:, 1:2], EXPERTS)
    margin = jnp.sum(logits * hot, axis=1, keepdims=True)
    gate[...] = jnp.broadcast_to(jax.nn.sigmoid(margin), (TOK, 128))


def send_rows(group, attn, resid, scale, shift, router, ids, place):
    return staged(
        norm_body,
        [group],
        [*attn, resid, scale, shift, router, ids, place],
        [
            hbm((EXPERTS, PLAIN, 128), BF),
            hbm((TOK, D), BF),
            hbm((TOK, 128), F32),
            hbm((TOK, 128), F32),
        ],
        "norm_dispatch",
        3,
        scratch=[
            pltpu.VMEM((TOK, D), F32),
            pltpu.VMEM((EXPERTS * PLAIN, 128), F32),
            pltpu.VMEM((SLOTS, D), F32),
        ],
    )


def gelu_terms(pre):
    square = pre * pre
    turn = jnp.tanh(GELU_C * (pre + 0.044715 * pre * square))
    return square, turn


def forward_body(arrived, w_in, w_out, after, rows, pre_out, y_send, stage, y_sum):
    step = pl.program_id(0)

    @pl.when(step == 0)
    def _():
        from_blocks(arrived, stage, rows, PLAIN)
        y_sum[...] = jnp.zeros_like(y_sum)

    pre = dot(rows[...], w_in[0])
    pre_out[0] = pre
    _, turn = gelu_terms(pre)
    act = (0.5 * pre * (1.0 + turn)).astype(BF)
    y_sum[...] += dot(act, w_out[0]).astype(BF).astype(F32)

    @pl.when(step == CTX - 1)
    def _():
        ref_to_blocks(y_sum, stage)
        store_blocks(stage, y_send)


def whole(*dims):
    return pl.BlockSpec(dims, lambda b: (0,) * len(dims))


def of_block(*dims):
    return pl.BlockSpec((1,) + dims, lambda b: (b,) + (0,) * len(dims))


def experts_forward(arrived, w_in, w_out, after):
    return pl.pallas_call(
        forward_body,
        grid=(CTX,),
        in_specs=[whole(EXPERTS, PLAIN, 128), of_block(D, FF_BLOCK), of_block(FF_BLOCK, D), IN_HBM],
        out_specs=[whole(SLOTS, D), of_block(SLOTS, FF_BLOCK), whole(EXPERTS, PLAIN, 128)],
        out_shape=[
            hbm((SLOTS, D), BF),
            hbm((CTX, SLOTS, FF_BLOCK), F32),
            hbm((EXPERTS, PLAIN, 128), BF),
        ],
        scratch_shapes=[pltpu.VMEM((EXPERTS * PLAIN, 128), F32), pltpu.VMEM((SLOTS, D), F32)],
        compiler_params=params(60),
        cost_estimate=cost(10),
        name="expert_forward",
    )(arrived, w_in, w_out, after)


def backward_body(
    rows, arrived_grads, pre_in, w_in, w_out, router, own,
    in_send, out_send, part_send,
    stage, part_sum, branch_grad, row_grads,
):
    step = pl.program_id(0)

    @pl.when(step == 0)
    def _():
        from_blocks(arrived_grads.at[:, 0:PLAIN, :], stage, branch_grad, PLAIN)
        partner_table = arrived_grads[:, PLAIN : PLAIN + 16, :].astype(F32)[:, 0, :]
        partner = jnp.concatenate(
            [partner_table[:, s : s + 1] for s in range(CAP)], axis=0
        ).astype(jnp.int32)
        logits = dot_cols(rows[...], router[...])
        margin = jnp.sum(logits * (own[...] - one_hot(partner, EXPERTS)), axis=1, keepdims=True)
        row_grads[...] = (jax.nn.sigmoid(margin) * branch_grad[...].astype(F32)).astype(BF)
        part_sum[...] = jnp.zeros_like(part_sum)

    pre = pre_in[0]
    square, turn = gelu_terms(pre)
    act = (0.5 * pre * (1.0 + turn)).astype(BF)
    slope = 0.5 * (1.0 + turn) + 0.5 * pre * (1.0 - turn * turn) * (
        GELU_C * (1.0 + 3.0 * 0.044715 * square)
    )
    pre_grad = (dot_cols(row_grads[...], w_out[0]) * slope).astype(BF)
    part_sum[...] += dot_cols(pre_grad, w_in[0]).astype(BF).astype(F32)
    in_send[0] = dot_rows(rows[...], pre_grad).astype(BF)
    out_send[0] = dot_rows(act, row_grads[...]).astype(BF)

    @pl.when(step == CTX - 1)
    def _():
        ref_to_blocks(part_sum, stage)
        store_blocks(stage, part_send.at[:, 0:PLAIN, :])
        part_send[:, PLAIN:, :] = jnp.zeros((EXPERTS, CHUNKS, 128), BF)


def experts_backward(rows, arrived_grads, pre, w_in, w_out, router, own):
    return pl.pallas_call(
        backward_body,
        grid=(CTX,),
        in_specs=[
            whole(SLOTS, D),
            whole(EXPERTS, TAGGED, 128),
            of_block(SLOTS, FF_BLOCK),
            of_block(D, FF_BLOCK),
            of_block(FF_BLOCK, D),
            whole(EXPERTS, D),
            whole(1, EXPERTS),
        ],
        out_specs=[of_block(D, FF_BLOCK), of_block(FF_BLOCK, D), whole(EXPERTS, TAGGED, 128)],
        out_shape=[
            hbm((CTX, D, FF_BLOCK), BF),
            hbm((CTX, FF_BLOCK, D), BF),
            hbm((EXPERTS, TAGGED, 128), BF),
        ],
        scratch_shapes=[
            pltpu.VMEM((EXPERTS * PLAIN, 128), F32),
            pltpu.VMEM((SLOTS, D), F32),
            pltpu.VMEM((SLOTS, D), BF),
            pltpu.VMEM((SLOTS, D), BF),
        ],
        compiler_params=params(60),
        cost_estimate=cost(15),
        name="expert_backward",
    )(rows, arrived_grads, pre, w_in, w_out, router, own)


def one_hots(ids):
    return one_hot(ids[:, 0:1], EXPERTS), one_hot(ids[:, 1:2], EXPERTS)


def resid_body(
    group, arrived, attn_0, attn_1, attn_2, attn_3, resid, grad_out, scale, router, place, logit_grad, inverse,
    resid_grad, router_column, send_0, send_1, send_2, send_3,
    stage, back, normed, lifted,
):
    from_blocks(arrived.at[:, 0:PLAIN, :], stage, back, PLAIN)
    router_column[...] = jnp.sum(arrived[:, PLAIN:TAGGED, :].astype(F32), axis=0)
    pick = (one_hot(place[:, 0:1], SLOTS) + one_hot(place[:, 1:2], SLOTS)).astype(BF)
    input_grad = dot(pick, back[...]) + dot(logit_grad[...], router[...])
    inv = inverse[:, 0:1]
    lifted[...] = input_grad * (1.0 + scale[...])
    mean = jnp.zeros((TOK, 1), F32)
    for s, attn in enumerate((attn_0, attn_1, attn_2, attn_3)):
        cols = group_cols(group, s)
        part = (resid[:, cols].astype(F32) + attn[...].astype(F32)) * inv
        normed[:, cols] = part
        mean = mean + jnp.sum(part * lifted[:, cols], axis=1, keepdims=True)
    mean = mean / D
    for s, send in enumerate((send_0, send_1, send_2, send_3)):
        cols = group_cols(group, s)
        part = grad_out[:, cols].astype(F32) + inv * (lifted[:, cols] - normed[:, cols] * mean)
        low_part = part.astype(BF)
        resid_grad[:, cols] = low_part
        send[...] = low_part


def resid_back(group, arrived, attn, resid, grad_out, scale, router, place, logit_grad, inverse):
    return staged(
        resid_body,
        [group],
        [arrived, *attn, resid, grad_out, scale, router, place, logit_grad, inverse],
        [hbm((TOK, D), BF), hbm((CHUNKS, 128), F32)] + [hbm((TOK, WIDE), BF)] * CTX,
        "resid_backward",
        30,
        scratch=[
            pltpu.VMEM((EXPERTS * PLAIN, 128), F32),
            pltpu.VMEM((SLOTS, D), BF),
            pltpu.VMEM((TOK, D), F32),
            pltpu.VMEM((TOK, D), F32),
        ],
        mib=60,
    )


def mixed_body(
    group, arrived, attn_0, attn_1, attn_2, attn_3, resid, grad_out, mod_gate, ids, place, gate, kept,
    out, logit_out, part_send,
    stage, back, branch, terms_blocks, sent_terms, sent,
):
    from_blocks(arrived, stage, back, PLAIN)
    gate_one = gate[:, 0:1]
    branch_grad = mod_gate[...] * grad_out[...].astype(F32)
    result_one = dot(one_hot(place[:, 0:1], SLOTS).astype(BF), back[...])
    pull = jnp.sum(branch_grad * result_one, axis=1, keepdims=True)
    result_two = dot(one_hot(place[:, 1:2], SLOTS).astype(BF), back[...])
    pull = pull - jnp.sum(branch_grad * result_two, axis=1, keepdims=True)
    first_hot, second_hot = one_hots(ids)
    tilt = pull * gate_one * (1.0 - gate_one)
    logit_grad = (tilt * (first_hot - second_hot)).astype(BF)
    logit_out[...] = logit_grad
    terms = dot_rows(logit_grad, kept[...])
    for c in range(CHUNKS):
        terms_blocks[pl.ds(c, EXPERTS, stride=CHUNKS), :] = terms[:, c * 128 : (c + 1) * 128]
    sent_terms[...] = terms_blocks[...].reshape(EXPERTS, CHUNKS, 128).astype(BF)
    copy = pltpu.make_async_copy(sent_terms, part_send.at[:, PLAIN:TAGGED, :], sent.at[0])
    copy.start()
    branch[...] = mod_gate[...] * (gate_one * result_one + (1.0 - gate_one) * result_two)
    for s, attn in enumerate((attn_0, attn_1, attn_2, attn_3)):
        cols = group_cols(group, s)
        hidden = resid[:, cols].astype(F32) + attn[...].astype(F32)
        out[:, cols] = (hidden + branch[:, cols]).astype(BF)
    copy.wait()


def mix(group, arrived, attn, resid, grad_out, mod_gate, ids, place, gate, kept, part_rows):
    return staged(
        mixed_body,
        [group],
        [arrived, *attn, resid, grad_out, mod_gate, ids, place, gate, kept],
        [hbm((TOK, D), BF), hbm((TOK, EXPERTS), BF)],
        "mixed_output",
        5,
        scratch=[
            pltpu.VMEM((EXPERTS * PLAIN, 128), F32),
            pltpu.VMEM((SLOTS, D), BF),
            pltpu.VMEM((TOK, D), F32),
            pltpu.VMEM((EXPERTS * CHUNKS, 128), F32),
            pltpu.VMEM((EXPERTS, CHUNKS, 128), BF),
            pltpu.SemaphoreType.DMA((1,)),
        ],
        mib=60,
        carried=part_rows,
    )


def order_body(blocks, out, stage):
    stage[...] = blocks[...].reshape(EXPERTS * CHUNKS, 128)
    for c in range(CHUNKS):
        out[:, c * 128 : (c + 1) * 128] = stage[pl.ds(c, EXPERTS, stride=CHUNKS), :]


def order_router(blocks):
    return staged(
        order_body,
        [],
        [blocks],
        hbm((EXPERTS, D), F32),
        "order_router",
        2,
        scratch=[pltpu.VMEM((EXPERTS * CHUNKS, 128), F32)],
    )


def swap(x):
    return lax.all_to_all(x, "expert", split_axis=0, concat_axis=0, tiled=True)


def shift(x, axis, count, step):
    return lax.ppermute(x, axis, [(i, (i + step) % count) for i in range(count)])


def around(parts, sign):
    return [parts[0]] + [shift(parts[s], "ctx", CTX, sign * s) for s in range(1, CTX)]


def local(
    resid, queries, keys, values, mod_scale, mod_shift, mod_gate, router, w_in, w_out, expert_ids, grad_out
):
    group = lax.axis_index("ctx").astype(jnp.int32)[None]
    expert = lax.axis_index("expert").astype(jnp.int32)
    own = (jnp.arange(EXPERTS, dtype=jnp.int32) == expert).astype(F32)[None, :]
    router_rows = router.T
    packed = pack(group, queries, keys, values)
    heads = around(packed, 1)
    place, grads = send_grads(grad_out, mod_gate, expert_ids, packed[0])
    arrived_grads = swap(grads)
    full_in = lax.all_gather(w_in, "ctx", axis=0, tiled=True)
    full_out = lax.all_gather(w_out, "ctx", axis=0, tiled=True)
    *attn_heads, saved = attend(heads)
    attn = around(attn_heads, -1)
    rows, kept, gate, inverse = send_rows(
        group, attn, resid, mod_scale, mod_shift, router_rows, expert_ids, place
    )
    arrived = swap(rows)
    flat_rows, pre_act, y_rows = experts_forward(arrived, full_in, full_out, arrived_grads)
    outputs = swap(y_rows)
    in_terms, out_terms, part_rows = experts_backward(
        flat_rows, arrived_grads, pre_act, full_in, full_out, router_rows, own
    )
    in_terms, out_terms, _ = lax.optimization_barrier((in_terms, out_terms, outputs))
    grad_w_in, grad_w_out = (
        lax.psum_scatter(x, "ctx", scatter_dimension=0, tiled=True) for x in (in_terms, out_terms)
    )
    mixed_out, logit_grad, part_rows = mix(
        group, outputs, attn, resid, grad_out, mod_gate, expert_ids, place, gate, kept, part_rows
    )
    parts = swap(part_rows)
    resid_grad, router_column, *head_grads = resid_back(
        group, parts, attn, resid, grad_out, mod_scale, router_rows, place, logit_grad, inverse
    )
    attn_grads = around(head_grads, 1)
    head_terms = attend_back(saved, attn_grads)
    head_sums = around(head_terms, -1)
    router_column, *_ = lax.optimization_barrier((router_column, *attn_grads[1:]))
    *columns, _ = lax.optimization_barrier((*around([router_column] * CTX, 1), head_terms[0]))
    router_column = columns[0] + columns[1] + columns[2] + columns[3]
    grad_router = order_router(
        swap(jnp.broadcast_to(router_column, (EXPERTS, CHUNKS, 128)))
    ).T
    grad_queries, grad_keys, grad_values = unpack(group, head_sums)
    return (
        mixed_out,
        resid_grad,
        grad_queries,
        grad_keys,
        grad_values,
        grad_w_in,
        grad_w_out,
        grad_router,
    )


def solution(mesh):
    tokens = P(("expert", "ctx"), None)
    clip = P("expert", None)
    return jax.shard_map(
        local,
        mesh=mesh,
        in_specs=(
            tokens, tokens, tokens, tokens, clip, clip, clip, P(),
            P("expert", None, "ctx"), P("expert", "ctx", None), tokens, tokens,
        ),
        out_specs=(
            tokens, tokens, tokens, tokens, tokens,
            P("expert", None, "ctx"), P("expert", "ctx", None), P(),
        ),
        check_vma=False,
    )
```
